32 devices in a mesh: row: 8 (over z, x), col: 4 (over y, core).
Axes of the slice: x: 2, y: 2, z: 4, core: 2. Of those that a mesh axis runs over, the one named last changes fastest.
Arguments:
- covariance: float32 [4096, 4096], P('row', 'col'), may hold values from -6 to 6
- left_ops: float32 [8, 3, 512, 512], P('row', None, None, 'col'), may hold values from -0.15625 to 0.15625
- right_ops: float32 [8, 3, 512, 512], P('col', None, 'row'), may hold values from -0.15625 to 0.15625
- edge_rows: float32 [2, 512, 4096], P(None, 'row', 'col'), may hold values from -6 to 6
- edge_cols: float32 [4096, 2, 512], P('row', None, 'col'), may hold values from -6 to 6
Outputs:
- forecast: float32 [4096, 4096], P('row', 'col')
The draws below stay inside these ranges and needn't reach their ends.
All inputs are finite; a program needn't handle non-finite values.
Results may differ from the reference program's by a relative error of at most 0.0003.
Values sent between devices are 32-bit elements; how exact they have to be, the bound alone decides.
A program may use at most 64 MiB of HBM per device.

```python
import jax
import jax.numpy as jnp
from jax import lax

BLK = 512
NB = 8
NW = 4096


def block_levels(stream_key, dims, split, low, top_value):
    def one(axis_at, shards_of):
        draws = jax.random.uniform(jax.random.fold_in(jax.random.fold_in(stream_key, 6), axis_at), (shards_of,), jnp.float32, low / len(split), top_value / len(split))
        return jnp.repeat(jnp.exp(draws), dims[axis_at] // shards_of).reshape((-1,) + (1,) * (len(dims) - axis_at - 1))

    gain = one(*split[0])
    for cut in split[1:]:
        gain = gain * one(*cut)
    return gain


def noise(stream_key, dims, width, reach, split=(), kind=jnp.bfloat16):
    result = width * jax.random.normal(stream_key, dims, jnp.float32)
    if split:
        result = result * block_levels(stream_key, dims, split, -0.22, 0.18)
    return jnp.clip(result, -reach, reach).astype(kind)


def setup_inputs(seed: int = 0) -> dict:
    splits = jax.random.split(jax.random.key(seed), 6)
    covariance = noise(splits[0], (NW, NW), 1.0, 6.0, ((0, 8), (1, 4)), jnp.float32)
    left_ops = noise(splits[1], (NB, 3, BLK, BLK), (3 * BLK) ** -0.5, 0.15625, ((0, 8), (3, 4)), jnp.float32)
    right_ops = noise(splits[2], (NB, 3, BLK, BLK), (3 * BLK) ** -0.5, 0.15625, ((0, 4), (2, 8)), jnp.float32)
    edge_rows = noise(splits[3], (2, BLK, NW), 1.0, 6.0, ((1, 8), (2, 4)), jnp.float32)
    edge_cols = noise(splits[4], (NW, 2, BLK), 1.0, 6.0, ((0, 8), (2, 4)), jnp.float32)
    return {"covariance": covariance, "left_ops": left_ops, "right_ops": right_ops, "edge_rows": edge_rows, "edge_cols": edge_cols}


def reference(covariance, left_ops, right_ops, edge_rows, edge_cols):
    rows_ext = jnp.concatenate([edge_rows[0], covariance, edge_rows[1]], axis=0)

    def row_band(index):
        window = lax.dynamic_slice_in_dim(rows_ext, (index * BLK).astype(jnp.int32), 3 * BLK, 0)
        blocks = lax.dynamic_index_in_dim(left_ops, index.astype(jnp.int32), 0, keepdims=False)
        wide = jnp.transpose(blocks, (1, 0, 2)).reshape(BLK, 3 * BLK)
        return jnp.dot(wide, window, preferred_element_type=jnp.float32, precision=lax.Precision.HIGHEST)

    half = lax.map(row_band, jnp.arange(NB, dtype=jnp.int32)).reshape(NW, NW)
    cols_ext = jnp.concatenate([edge_cols[:, 0, :], half, edge_cols[:, 1, :]], axis=1)

    def col_band(index):
        window = lax.dynamic_slice_in_dim(cols_ext, (index * BLK).astype(jnp.int32), 3 * BLK, 1)
        blocks = lax.dynamic_index_in_dim(right_ops, index.astype(jnp.int32), 0, keepdims=False)
        wide = jnp.transpose(blocks, (1, 0, 2)).reshape(BLK, 3 * BLK)
        return jnp.dot(window, wide.T, preferred_element_type=jnp.float32, precision=lax.Precision.HIGHEST)

    bands = lax.map(col_band, jnp.arange(NB, dtype=jnp.int32))
    return jnp.transpose(bands, (1, 0, 2)).reshape(NW, NW)
```

```python
import functools

import jax
import jax.numpy as jnp
from jax import lax
from jax.experimental import pallas as pl
from jax.experimental.pallas import tpu as pltpu
from jax.sharding import PartitionSpec as P

F32, BF16 = jnp.float32, jnp.bfloat16
TILE = 256
CHUNKS = 4


def halves(value):
    high = value.astype(BF16)
    return high, (value - high.astype(F32)).astype(BF16)


def product(a_high, a_low, b_high, b_low, transposed):
    dims = (((1,), (1 if transposed else 0,)), ((), ()))
    dot = functools.partial(lax.dot_general, dimension_numbers=dims, preferred_element_type=F32)
    return dot(a_high, b_high) + (dot(a_high, b_low) + dot(a_low, b_high))


def kernel(
    rows, cols, cov, left, right, edge_r, edge_c, out,
    near, left_all, right_all, edge_all, half, halo, l_high, l_low, w_high, w_low,
    c_send, c_recv, f_send, f_recv, l_send, l_recv, rz_send, rp_send, r_recv, er_send, er_recv,
    ec_send, ec_recv, h_send, h_recv, own_sem,
):
    i, c = lax.axis_index("row"), lax.axis_index("col")
    block = cov.shape[0]
    bands = right.shape[0]
    part = right.shape[2]
    depth = rows // 2
    odd = lax.rem(i, 2)
    pair = i + 1 - 2 * odd
    onward = i + 2 - 4 * odd
    has_onward = (onward >= 0) & (onward < rows)
    fed = (i - 2 + 4 * odd >= 0) & (i - 2 + 4 * odd < rows)
    step_rows = block // CHUNKS

    def remote(src, dst, send, recv, row=None, col=None):
        target = (i if row is None else row, c if col is None else col)
        return pltpu.make_async_remote_copy(
            src_ref=src, dst_ref=dst, send_sem=send, recv_sem=recv,
            device_id=target, device_id_type=pl.DeviceIdType.MESH,
        )

    barrier = pltpu.get_barrier_semaphore()
    for k in range(1, rows):
        pl.semaphore_signal(
            barrier, inc=1, device_id=(lax.rem(i + k, rows), c), device_id_type=pl.DeviceIdType.MESH
        )
    for k in range(1, cols):
        pl.semaphore_signal(
            barrier, inc=1, device_id=(i, lax.rem(c + k, cols)), device_id_type=pl.DeviceIdType.MESH
        )
    pl.semaphore_wait(barrier, rows + cols - 2)

    def piece(j, r):
        return right_all.at[j, :, pl.ds(pl.multiple_of(r * part, part), part), :]

    def cov_copy(k):
        rng = pl.ds(k * step_rows, step_rows)
        return remote(cov.at[rng], near.at[odd, rng], c_send.at[k], c_recv.at[k], row=pair)

    def cov_arrive(k):
        rng = pl.ds(k * step_rows, step_rows)
        return remote(cov.at[rng], near.at[1 - odd, rng], c_send.at[k], c_recv.at[k], row=pair)

    def far_copy(k):
        rng = pl.ds(k * step_rows, step_rows)
        return remote(near.at[1 - odd, rng], near.at[odd, rng], f_send.at[k], f_recv.at[k], row=onward)

    def r_copy_z(j, d, way, r, src):
        return remote(src, piece(j, r), rz_send.at[j, way, d], r_recv.at[j, r], row=i + (2 if way else -2))

    def r_copy_p(j, slot, r, src):
        return remote(src, piece(j, r), rp_send.at[j, slot], r_recv.at[j, r], row=pair)

    for k in range(CHUNKS):
        cov_copy(k).start()
    up, down = i + 2 < rows, i - 2 >= 0
    for j in range(bands):
        @pl.when(up)
        def _():
            r_copy_z(j, 0, 1, i, right.at[j]).start()

        @pl.when(down)
        def _():
            r_copy_z(j, 0, 0, i, right.at[j]).start()

    def l_copy(k):
        return remote(left.at[0], left_all.at[c], l_send.at[k], l_recv.at[c], col=lax.rem(c + k, cols))

    for k in range(1, cols):
        l_copy(k).start()
    er0 = remote(
        edge_r.at[0], near.at[0, pl.ds(pl.multiple_of(i * part, part), part)],
        er_send.at[0], er_recv.at[i], row=0,
    )
    er1 = remote(
        edge_r.at[1], near.at[1, pl.ds(pl.multiple_of(i * part, part), part)],
        er_send.at[1], er_recv.at[i], row=rows - 1,
    )
    ec0 = remote(edge_c.at[0], edge_all.at[c], ec_send.at[0], ec_recv.at[c], col=0)
    ec1 = remote(edge_c.at[1], edge_all.at[c], ec_send.at[1], ec_recv.at[c], col=cols - 1)

    @pl.when(i != 0)
    def _():
        er0.start()

    @pl.when(i != rows - 1)
    def _():
        er1.start()

    @pl.when(c != 0)
    def _():
        ec0.start()

    @pl.when(c != cols - 1)
    def _():
        ec1.start()

    for j in range(bands):
        r_copy_p(j, 0, i, right.at[j]).start()

    own = [pltpu.make_async_copy(left.at[0], left_all.at[c], own_sem.at[0])]
    own += [pltpu.make_async_copy(right.at[j], piece(j, i), own_sem.at[1 + j]) for j in range(bands)]
    for copy in own:
        copy.start()

    @pl.when(i == 0)
    def _():
        near[0, :part] = edge_r[0]

    @pl.when(i == rows - 1)
    def _():
        near[1, (rows - 1) * part :] = edge_r[1]

    @pl.when(c == 0)
    def _():
        edge_all[0] = edge_c[0]

    @pl.when(c == cols - 1)
    def _():
        edge_all[cols - 1] = edge_c[1]

    def pass_on(d):
        for j in range(bands):
            for way in (1, 0):
                r = i - 2 * d if way else i + 2 * d

                @pl.when((r >= 0) & (r < rows))
                def _():
                    r_copy_z(j, d, way, r, piece(j, r)).wait_recv()

                    @pl.when(up if way else down)
                    def _():
                        r_copy_z(j, d, way, r, piece(j, r)).start()

                    r_copy_p(j, 2 * d - way, r, piece(j, r)).start()

    for k in range(CHUNKS):
        cov_arrive(k).wait_recv()

        @pl.when(has_onward)
        def _():
            far_copy(k).start()

        if k == 1 and depth > 1:
            pass_on(1)

    for copy in own:
        copy.wait()
    for k in range(1, cols):
        source = lax.rem(c + k, cols)
        remote(left.at[0], left_all.at[source], l_send.at[k], l_recv.at[source], col=source).wait_recv()
    width = left_all.shape[3]
    for k in range(cols):
        for m in range(3):
            high, low = halves(left_all[k, m])
            l_high[m, :, k * width : (k + 1) * width] = high
            l_low[m, :, k * width : (k + 1) * width] = low

    per_band = block // TILE

    def left_product(m, source, t):
        high, low = halves(source)
        return product(l_high[m], l_low[m], high, low, False)

    def tile_of(t):
        return t // per_band, pl.ds(pl.multiple_of(lax.rem(t, per_band) * TILE, TILE), TILE)

    @pl.loop(0, bands * per_band)
    def _(t):
        band, span = tile_of(t)
        flat = pl.ds(pl.multiple_of(t * TILE, TILE), TILE)
        half[band, :, span] = left_product(1, cov[:, flat], t)

    if depth > 2:
        pass_on(2)

    @pl.loop(0, bands * per_band)
    def _(t):
        band, span = tile_of(t)
        flat = pl.ds(pl.multiple_of(t * TILE, TILE), TILE)
        half[band, :, span] += left_product(2 - 2 * odd, near[1 - odd, :, flat], t)

    @pl.when(fed)
    def _():
        for k in range(CHUNKS):
            rng = pl.ds(k * step_rows, step_rows)
            remote(cov.at[rng], near.at[odd, rng], f_send.at[k], f_recv.at[k], row=pair).wait_recv()

    @pl.when(jnp.logical_not(fed))
    def _():
        for k in range(1, rows):
            source = lax.rem(i + k, rows)
            remote(
                edge_r.at[0], near.at[odd, pl.ds(pl.multiple_of(source * part, part), part)],
                er_send.at[0], er_recv.at[source], row=source,
            ).wait_recv()

    @pl.loop(0, bands * per_band)
    def _(t):
        band, span = tile_of(t)
        flat = pl.ds(pl.multiple_of(t * TILE, TILE), TILE)
        total = half[band, :, span] + left_product(2 * odd, near[odd, :, flat], t)
        half[band, :, span] = total
        high, low = halves(total)
        w_high[band + 1, :, span] = high
        w_low[band + 1, :, span] = low

    to_right = remote(half.at[bands - 1], halo.at[0], h_send.at[0], h_recv.at[0], col=c + 1)
    to_left = remote(half.at[0], halo.at[1], h_send.at[1], h_recv.at[1], col=c - 1)

    @pl.when(c < cols - 1)
    def _():
        to_right.start()

    @pl.when(c > 0)
    def _():
        to_left.start()

    for d in range(3, depth):
        pass_on(d)

    def store_halo(side, inner, copy):
        at = side * (bands + 1)

        @pl.when(inner)
        def _():
            copy.wait_recv()
            high, low = halves(halo[side])
            w_high[at] = high
            w_low[at] = low

        @pl.when(jnp.logical_not(inner))
        def _():
            for k in range(1, cols):
                source = lax.rem(c + k, cols)
                remote(
                    edge_c.at[0], edge_all.at[source], ec_send.at[0], ec_recv.at[source], col=source
                ).wait_recv()
            for k in range(cols):
                high, low = halves(edge_all[k])
                w_high[at, :, k * width : (k + 1) * width] = high
                w_low[at, :, k * width : (k + 1) * width] = low

    store_halo(0, c > 0, to_right)
    store_halo(1, c < cols - 1, to_left)

    for j in range(bands):
        for z in range(depth):
            r = 2 * z + 1 - odd
            r_copy_p(j, 0, r, piece(j, r)).wait_recv()

        @pl.loop(0, per_band)
        def _(t):
            span = pl.ds(pl.multiple_of(t * TILE, TILE), TILE)
            total = None
            for m in range(3):
                high, low = halves(right_all[j, m, span, :])
                term = product(w_high[j + m], w_low[j + m], high, low, True)
                total = term if total is None else total + term
            out[:, pl.ds(pl.multiple_of(j * block + t * TILE, TILE), TILE)] = total

    for k in range(CHUNKS):
        cov_copy(k).wait_send()

        @pl.when(has_onward)
        def _():
            far_copy(k).wait_send()

    for k in range(1, cols):
        l_copy(k).wait_send()
    for j in range(bands):
        r_copy_p(j, 0, i, right.at[j]).wait_send()
        for d in range(depth):
            for way in (1, 0):
                r = i - 2 * d if way else i + 2 * d

                @pl.when((r >= 0) & (r < rows))
                def _():
                    @pl.when(up if way else down)
                    def _():
                        r_copy_z(j, d, way, r, piece(j, r)).wait_send()

                    if d:
                        r_copy_p(j, 2 * d - way, r, piece(j, r)).wait_send()

    @pl.when(i != 0)
    def _():
        er0.wait_send()

    @pl.when(i != rows - 1)
    def _():
        er1.wait_send()

    @pl.when(c != 0)
    def _():
        ec0.wait_send()

    @pl.when(c != cols - 1)
    def _():
        ec1.wait_send()

    @pl.when(c < cols - 1)
    def _():
        to_right.wait_send()

    @pl.when(c > 0)
    def _():
        to_left.wait_send()


def solution(mesh):
    rows, cols = mesh.shape["row"], mesh.shape["col"]

    def on_device(covariance, left_ops, right_ops, edge_rows, edge_cols):
        block = covariance.shape[0]
        bands, _, part, _ = right_ops.shape
        width = left_ops.shape[3]
        edge_cols = jnp.transpose(edge_cols, (1, 0, 2))
        dma = pltpu.SemaphoreType.DMA
        depth = rows // 2
        return pl.pallas_call(
            functools.partial(kernel, rows, cols),
            out_shape=jax.ShapeDtypeStruct(covariance.shape, F32),
            in_specs=[pl.BlockSpec(memory_space=pltpu.VMEM)] * 5,
            out_specs=pl.BlockSpec(memory_space=pltpu.VMEM),
            scratch_shapes=[
                pltpu.VMEM((2,) + covariance.shape, F32),
                pltpu.VMEM((cols, 3, block, width), F32),
                pltpu.VMEM((bands, 3, block, block), F32),
                pltpu.VMEM((cols, block, width), F32),
                pltpu.VMEM((bands, block, block), F32),
                pltpu.VMEM((2, block, block), F32),
                pltpu.VMEM((3, block, block), BF16),
                pltpu.VMEM((3, block, block), BF16),
                pltpu.VMEM((bands + 2, block, block), BF16),
                pltpu.VMEM((bands + 2, block, block), BF16),
                dma((CHUNKS,)), dma((CHUNKS,)), dma((CHUNKS,)), dma((CHUNKS,)),
                dma((cols,)), dma((cols,)),
                dma((bands, 2, depth)), dma((bands, 2 * depth)), dma((bands, rows)),
                dma((2,)), dma((rows,)), dma((2,)), dma((cols,)), dma((2,)), dma((2,)),
                dma((1 + bands,)),
            ],
            compiler_params=pltpu.CompilerParams(
                collective_id=0, has_side_effects=True, vmem_limit_bytes=63 * 1024 * 1024
            ),
        )(covariance, left_ops, right_ops, edge_rows, edge_cols)

    return jax.shard_map(
        on_device,
        mesh=mesh,
        in_specs=(
            P("row", "col"),
            P("row", None, None, "col"),
            P("col", None, "row", None),
            P(None, "row", "col"),
            P("row", None, "col"),
        ),
        out_specs=P("row", "col"),
        check_vma=False,
    )
```

```python
import functools

import jax
import jax.numpy as jnp
from jax import lax
from jax.experimental import pallas as pl
from jax.experimental.pallas import tpu as pltpu
from jax.sharding import PartitionSpec as P

F32, BF16 = jnp.float32, jnp.bfloat16
TILE = 256
CHUNKS = 4


def halves(value):
    high = value.astype(BF16)
    return high, (value - high.astype(F32)).astype(BF16)


def product(a_high, a_low, b_high, b_low, transposed):
    dims = (((1,), (1 if transposed else 0,)), ((), ()))
    dot = functools.partial(lax.dot_general, dimension_numbers=dims, preferred_element_type=F32)
    return dot(a_high, b_high) + (dot(a_high, b_low) + dot(a_low, b_high))


def kernel(
    rows, cols, cov, left, right, edge_r, edge_c, out,
    near, left_all, right_all, edge_all, half, halo, relay, l_high, l_low, w_high, w_low,
    c_send, c_recv, f_send, f_recv, l_send, l_recv, rz_send, rp_send, r_recv, er_send, er_recv, ex_send, ex_recv,
    ec_send, ec_recv, h_send, h_recv, own_sem,
):
    i, c = lax.axis_index("row"), lax.axis_index("col")
    block = cov.shape[0]
    bands = right.shape[0]
    part = right.shape[2]
    depth = rows // 2
    odd = lax.rem(i, 2)
    pair = i + 1 - 2 * odd
    onward = i + 2 - 4 * odd
    has_onward = (onward >= 0) & (onward < rows)
    fed = (i - 2 + 4 * odd >= 0) & (i - 2 + 4 * odd < rows)
    step_rows = block // CHUNKS

    def remote(src, dst, send, recv, row=None, col=None):
        target = (i if row is None else row, c if col is None else col)
        return pltpu.make_async_remote_copy(
            src_ref=src, dst_ref=dst, send_sem=send, recv_sem=recv,
            device_id=target, device_id_type=pl.DeviceIdType.MESH,
        )

    barrier = pltpu.get_barrier_semaphore()
    for k in range(1, rows):
        pl.semaphore_signal(
            barrier, inc=1, device_id=(lax.rem(i + k, rows), c), device_id_type=pl.DeviceIdType.MESH
        )
    for k in range(1, cols):
        pl.semaphore_signal(
            barrier, inc=1, device_id=(i, lax.rem(c + k, cols)), device_id_type=pl.DeviceIdType.MESH
        )
    pl.semaphore_wait(barrier, rows + cols - 2)

    def piece(j, r):
        return right_all.at[j, :, pl.ds(pl.multiple_of(r * part, part), part), :]

    def cov_copy(k):
        rng = pl.ds(k * step_rows, step_rows)
        return remote(cov.at[rng], near.at[odd, rng], c_send.at[k], c_recv.at[k], row=pair)

    def cov_arrive(k):
        rng = pl.ds(k * step_rows, step_rows)
        return remote(cov.at[rng], near.at[1 - odd, rng], c_send.at[k], c_recv.at[k], row=pair)

    def far_copy(k):
        rng = pl.ds(k * step_rows, step_rows)
        return remote(near.at[1 - odd, rng], near.at[odd, rng], f_send.at[k], f_recv.at[k], row=onward)

    def r_copy_z(j, d, way, r, src):
        return remote(src, piece(j, r), rz_send.at[j, way, d], r_recv.at[j, r], row=i + (2 if way else -2))

    def r_copy_p(j, slot, r, src):
        return remote(src, piece(j, r), rp_send.at[j, slot], r_recv.at[j, r], row=pair)

    for k in range(CHUNKS):
        cov_copy(k).start()
    up, down = i + 2 < rows, i - 2 >= 0

    def own_z(j):
        @pl.when(up)
        def _():
            r_copy_z(j, 0, 1, i, right.at[j]).start()

        @pl.when(down)
        def _():
            r_copy_z(j, 0, 0, i, right.at[j]).start()

    own_z(0)
    ex = remote(edge_r.at[1 - odd], relay, ex_send.at[0], ex_recv.at[0], row=pair)
    ex.start()
    r_copy_p(0, 0, i, right.at[0]).start()

    def l_copy(k):
        return remote(left.at[0], left_all.at[c], l_send.at[k], l_recv.at[c], col=lax.rem(c + k, cols))

    for k in range(1, cols):
        l_copy(k).start()
    goal = odd * (rows - 1)

    def edge_copy(k, src, r):
        dst = near.at[odd, pl.ds(pl.multiple_of(r * part, part), part)]
        return remote(src, dst, er_send.at[k], er_recv.at[r], row=goal)

    ec0 = remote(edge_c.at[0], edge_all.at[c], ec_send.at[0], ec_recv.at[c], col=0)
    ec1 = remote(edge_c.at[1], edge_all.at[c], ec_send.at[1], ec_recv.at[c], col=cols - 1)

    @pl.when(c != 0)
    def _():
        ec0.start()

    @pl.when(c != cols - 1)
    def _():
        ec1.start()

    own = [pltpu.make_async_copy(left.at[0], left_all.at[c], own_sem.at[0])]
    own += [pltpu.make_async_copy(right.at[j], piece(j, i), own_sem.at[1 + j]) for j in range(bands)]
    for copy in own:
        copy.start()

    @pl.when(i == 0)
    def _():
        near[0, :part] = edge_r[0]

    @pl.when(i == rows - 1)
    def _():
        near[1, (rows - 1) * part :] = edge_r[1]

    @pl.when(c == 0)
    def _():
        edge_all[0] = edge_c[0]

    @pl.when(c == cols - 1)
    def _():
        edge_all[cols - 1] = edge_c[1]

    def pass_z(d, j):
        for way in (1, 0):
            r = i - 2 * d if way else i + 2 * d

            @pl.when((r >= 0) & (r < rows))
            def _():
                r_copy_z(j, d, way, r, piece(j, r)).wait_recv()

                @pl.when(up if way else down)
                def _():
                    r_copy_z(j, d, way, r, piece(j, r)).start()

    def pass_x(d, j):
        for way in (1, 0):
            r = i - 2 * d if way else i + 2 * d

            @pl.when((r >= 0) & (r < rows))
            def _():
                r_copy_p(j, 2 * d - way, r, piece(j, r)).start()

    def cov_on(k):
        cov_arrive(k).wait_recv()

        @pl.when(has_onward)
        def _():
            far_copy(k).start()

    taken = 0
    for d in range(1, depth):
        pass_z(d, 0)
        pass_x(d, 0)
        if d == 1:
            for j in range(1, bands):
                own_z(j)
        if d < depth - 1 and taken < CHUNKS - 2:
            cov_on(taken)
            taken += 1
    for j in range(1, bands):
        r_copy_p(j, 0, i, right.at[j]).start()
        if depth > 1:
            pass_z(1, j)
            pass_x(1, j)

    for k in range(taken, CHUNKS):
        cov_on(k)
    ex.wait_recv()

    @pl.when(i != goal)
    def _():
        edge_copy(0, edge_r.at[odd], i).start()
        edge_copy(1, relay, pair).start()

    @pl.when(i == 0)
    def _():
        near[0, part : 2 * part] = relay[...]

    @pl.when(i == rows - 1)
    def _():
        near[1, (rows - 2) * part : (rows - 1) * part] = relay[...]

    for copy in own:
        copy.wait()
    for k in range(1, cols):
        source = lax.rem(c + k, cols)
        remote(left.at[0], left_all.at[source], l_send.at[k], l_recv.at[source], col=source).wait_recv()
    width = left_all.shape[3]
    for k in range(cols):
        for m in range(3):
            high, low = halves(left_all[k, m])
            l_high[m, :, k * width : (k + 1) * width] = high
            l_low[m, :, k * width : (k + 1) * width] = low

    per_band = block // TILE

    def left_product(m, source, t):
        high, low = halves(source)
        return product(l_high[m], l_low[m], high, low, False)

    def tile_of(t):
        return t // per_band, pl.ds(pl.multiple_of(lax.rem(t, per_band) * TILE, TILE), TILE)

    @pl.loop(0, bands * per_band)
    def _(t):
        band, span = tile_of(t)
        flat = pl.ds(pl.multiple_of(t * TILE, TILE), TILE)
        half[band, :, span] = left_product(1, cov[:, flat], t)

    for j in range(1, bands):
        if depth > 2:
            pass_z(2, j)
            pass_x(2, j)

    @pl.loop(0, bands * per_band)
    def _(t):
        band, span = tile_of(t)
        flat = pl.ds(pl.multiple_of(t * TILE, TILE), TILE)
        half[band, :, span] += left_product(2 - 2 * odd, near[1 - odd, :, flat], t)

    @pl.when(fed)
    def _():
        for k in range(CHUNKS):
            rng = pl.ds(k * step_rows, step_rows)
            remote(cov.at[rng], near.at[odd, rng], f_send.at[k], f_recv.at[k], row=pair).wait_recv()

    @pl.when(jnp.logical_not(fed))
    def _():
        for k in range(rows - 2):
            edge_copy(0, edge_r.at[0], 2 - 2 * odd + k).wait_recv()

    @pl.loop(0, bands * per_band)
    def _(t):
        band, span = tile_of(t)
        flat = pl.ds(pl.multiple_of(t * TILE, TILE), TILE)
        total = half[band, :, span] + left_product(2 * odd, near[odd, :, flat], t)
        half[band, :, span] = total
        high, low = halves(total)
        w_high[band + 1, :, span] = high
        w_low[band + 1, :, span] = low

    to_right = remote(half.at[bands - 1], halo.at[0], h_send.at[0], h_recv.at[0], col=c + 1)
    to_left = remote(half.at[0], halo.at[1], h_send.at[1], h_recv.at[1], col=c - 1)

    @pl.when(c < cols - 1)
    def _():
        to_right.start()

    @pl.when(c > 0)
    def _():
        to_left.start()

    for d in range(3, depth):
        for j in range(1, bands):
            pass_z(d, j)
            pass_x(d, j)

    def store_halo(side, inner, copy):
        at = side * (bands + 1)

        @pl.when(inner)
        def _():
            copy.wait_recv()
            high, low = halves(halo[side])
            w_high[at] = high
            w_low[at] = low

        @pl.when(jnp.logical_not(inner))
        def _():
            for k in range(1, cols):
                source = lax.rem(c + k, cols)
                remote(
                    edge_c.at[0], edge_all.at[source], ec_send.at[0], ec_recv.at[source], col=source
                ).wait_recv()
            for k in range(cols):
                high, low = halves(edge_all[k])
                w_high[at, :, k * width : (k + 1) * width] = high
                w_low[at, :, k * width : (k + 1) * width] = low

    store_halo(0, c > 0, to_right)
    store_halo(1, c < cols - 1, to_left)

    for j in range(bands):
        for z in range(depth):
            r = 2 * z + 1 - odd
            r_copy_p(j, 0, r, piece(j, r)).wait_recv()

        @pl.loop(0, per_band)
        def _(t):
            span = pl.ds(pl.multiple_of(t * TILE, TILE), TILE)
            total = None
            for m in range(3):
                high, low = halves(right_all[j, m, span, :])
                term = product(w_high[j + m], w_low[j + m], high, low, True)
                total = term if total is None else total + term
            out[:, pl.ds(pl.multiple_of(j * block + t * TILE, TILE), TILE)] = total

    for k in range(CHUNKS):
        cov_copy(k).wait_send()

        @pl.when(has_onward)
        def _():
            far_copy(k).wait_send()

    for k in range(1, cols):
        l_copy(k).wait_send()
    for j in range(bands):
        r_copy_p(j, 0, i, right.at[j]).wait_send()
        for d in range(depth):
            for way in (1, 0):
                r = i - 2 * d if way else i + 2 * d

                @pl.when((r >= 0) & (r < rows))
                def _():
                    @pl.when(up if way else down)
                    def _():
                        r_copy_z(j, d, way, r, piece(j, r)).wait_send()

                    if d:
                        r_copy_p(j, 2 * d - way, r, piece(j, r)).wait_send()

    ex.wait_send()

    @pl.when(i != goal)
    def _():
        edge_copy(0, edge_r.at[odd], i).wait_send()
        edge_copy(1, relay, pair).wait_send()

    @pl.when(c != 0)
    def _():
        ec0.wait_send()

    @pl.when(c != cols - 1)
    def _():
        ec1.wait_send()

    @pl.when(c < cols - 1)
    def _():
        to_right.wait_send()

    @pl.when(c > 0)
    def _():
        to_left.wait_send()


def solution(mesh):
    rows, cols = mesh.shape["row"], mesh.shape["col"]

    def on_device(covariance, left_ops, right_ops, edge_rows, edge_cols):
        block = covariance.shape[0]
        bands, _, part, _ = right_ops.shape
        width = left_ops.shape[3]
        edge_cols = jnp.transpose(edge_cols, (1, 0, 2))
        dma = pltpu.SemaphoreType.DMA
        depth = rows // 2
        return pl.pallas_call(
            functools.partial(kernel, rows, cols),
            out_shape=jax.ShapeDtypeStruct(covariance.shape, F32),
            in_specs=[pl.BlockSpec(memory_space=pltpu.VMEM)] * 5,
            out_specs=pl.BlockSpec(memory_space=pltpu.VMEM),
            scratch_shapes=[
                pltpu.VMEM((2,) + covariance.shape, F32),
                pltpu.VMEM((cols, 3, block, width), F32),
                pltpu.VMEM((bands, 3, block, block), F32),
                pltpu.VMEM((cols, block, width), F32),
                pltpu.VMEM((bands, block, block), F32),
                pltpu.VMEM((2, block, block), F32),
                pltpu.VMEM((part, covariance.shape[1]), F32),
                pltpu.VMEM((3, block, block), BF16),
                pltpu.VMEM((3, block, block), BF16),
                pltpu.VMEM((bands + 2, block, block), BF16),
                pltpu.VMEM((bands + 2, block, block), BF16),
                dma((CHUNKS,)), dma((CHUNKS,)), dma((CHUNKS,)), dma((CHUNKS,)),
                dma((cols,)), dma((cols,)),
                dma((bands, 2, depth)), dma((bands, 2 * depth)), dma((bands, rows)),
                dma((2,)), dma((rows,)), dma((1,)), dma((1,)), dma((2,)), dma((cols,)), dma((2,)), dma((2,)),
                dma((1 + bands,)),
            ],
            compiler_params=pltpu.CompilerParams(
                collective_id=0, has_side_effects=True, vmem_limit_bytes=63 * 1024 * 1024
            ),
        )(covariance, left_ops, right_ops, edge_rows, edge_cols)

    return jax.shard_map(
        on_device,
        mesh=mesh,
        in_specs=(
            P("row", "col"),
            P("row", None, None, "col"),
            P("col", None, "row", None),
            P(None, "row", "col"),
            P("row", None, "col"),
        ),
        out_specs=P("row", "col"),
        check_vma=False,
    )
```

```python
import functools

import jax
import jax.numpy as jnp
from jax import lax
from jax.experimental import pallas as pl
from jax.experimental.pallas import tpu as pltpu
from jax.sharding import PartitionSpec as P

F32, BF16 = jnp.float32, jnp.bfloat16
TILE = 256
CHUNKS = 4


def halves(value):
    high = value.astype(BF16)
    return high, (value - high.astype(F32)).astype(BF16)


def product(a_high, a_low, b_high, b_low, transposed):
    dims = (((1,), (1 if transposed else 0,)), ((), ()))
    dot = functools.partial(lax.dot_general, dimension_numbers=dims, preferred_element_type=F32)
    return dot(a_high, b_high) + (dot(a_high, b_low) + dot(a_low, b_high))


def kernel(
    rows, cols, cov, left, right, edge_r, edge_c, out,
    near, left_all, right_all, edge_all, half, halo, relay, l_high, l_low, w_high, w_low,
    c_send, c_recv, f_send, f_recv, l_send, l_recv, rz_send, rp_send, r_recv, er_send, er_recv, ex_send, ex_recv,
    ec_send, ec_recv, h_send, h_recv, sx_send, sz_send, s_recv, own_sem,
):
    i, c = lax.axis_index("row"), lax.axis_index("col")
    block = cov.shape[0]
    bands = right.shape[0]
    part = right.shape[2]
    depth = rows // 2
    odd = lax.rem(i, 2)
    pair = i + 1 - 2 * odd
    onward = i + 2 - 4 * odd
    has_onward = (onward >= 0) & (onward < rows)
    fed = (i - 2 + 4 * odd >= 0) & (i - 2 + 4 * odd < rows)
    step_rows = block // CHUNKS

    def remote(src, dst, send, recv, row=None, col=None):
        target = (i if row is None else row, c if col is None else col)
        return pltpu.make_async_remote_copy(
            src_ref=src, dst_ref=dst, send_sem=send, recv_sem=recv,
            device_id=target, device_id_type=pl.DeviceIdType.MESH,
        )

    barrier = pltpu.get_barrier_semaphore()
    for k in range(1, rows):
        pl.semaphore_signal(
            barrier, inc=1, device_id=(lax.rem(i + k, rows), c), device_id_type=pl.DeviceIdType.MESH
        )
    for k in range(1, cols):
        pl.semaphore_signal(
            barrier, inc=1, device_id=(i, lax.rem(c + k, cols)), device_id_type=pl.DeviceIdType.MESH
        )
    pl.semaphore_wait(barrier, rows + cols - 2)

    last = bands - 1

    def span_of(r):
        return pl.ds(pl.multiple_of(r * part, part), part)

    def piece(j, r):
        return right_all.at[j, pl.ds(0, 2 if j == last else 3), span_of(r), :]

    def own_piece(j):
        return right.at[j, pl.ds(0, 2 if j == last else 3)]

    def side_piece(r):
        return right_all.at[last, 2, span_of(r), :]

    def s_copy_z(kind, d, way, r, src):
        return remote(
            src, side_piece(r), sz_send.at[kind, way, d], s_recv.at[r], row=i + (2 if way else -2)
        )

    def s_copy_x(r):
        return remote(right.at[last, 2], side_piece(r), sx_send.at[0], s_recv.at[r], row=pair)

    def cov_copy(k):
        rng = pl.ds(k * step_rows, step_rows)
        return remote(cov.at[rng], near.at[odd, rng], c_send.at[k], c_recv.at[k], row=pair)

    def cov_arrive(k):
        rng = pl.ds(k * step_rows, step_rows)
        return remote(cov.at[rng], near.at[1 - odd, rng], c_send.at[k], c_recv.at[k], row=pair)

    def far_copy(k):
        rng = pl.ds(k * step_rows, step_rows)
        return remote(near.at[1 - odd, rng], near.at[odd, rng], f_send.at[k], f_recv.at[k], row=onward)

    def r_copy_z(j, d, way, r, src):
        return remote(src, piece(j, r), rz_send.at[j, way, d], r_recv.at[j, r], row=i + (2 if way else -2))

    def r_copy_p(j, slot, r, src):
        return remote(src, piece(j, r), rp_send.at[j, slot], r_recv.at[j, r], row=pair)

    for k in range(CHUNKS):
        cov_copy(k).start()
    up, down = i + 2 < rows, i - 2 >= 0

    def own_z(j):
        @pl.when(up)
        def _():
            r_copy_z(j, 0, 1, i, own_piece(j)).start()

        @pl.when(down)
        def _():
            r_copy_z(j, 0, 0, i, own_piece(j)).start()

    own_z(0)
    ex = remote(edge_r.at[1 - odd], relay, ex_send.at[0], ex_recv.at[0], row=pair)
    ex.start()
    r_copy_p(0, 0, i, own_piece(0)).start()
    s_copy_x(i).start()

    def l_copy(k):
        return remote(left.at[0], left_all.at[c], l_send.at[k], l_recv.at[c], col=lax.rem(c + k, cols))

    for k in range(1, cols):
        l_copy(k).start()
    goal = odd * (rows - 1)

    def edge_copy(k, src, r):
        dst = near.at[odd, pl.ds(pl.multiple_of(r * part, part), part)]
        return remote(src, dst, er_send.at[k], er_recv.at[r], row=goal)

    ec0 = remote(edge_c.at[0], edge_all.at[c], ec_send.at[0], ec_recv.at[c], col=0)
    ec1 = remote(edge_c.at[1], edge_all.at[c], ec_send.at[1], ec_recv.at[c], col=cols - 1)

    @pl.when(c != 0)
    def _():
        ec0.start()

    @pl.when(c != cols - 1)
    def _():
        ec1.start()

    own = [pltpu.make_async_copy(left.at[0], left_all.at[c], own_sem.at[0])]
    own += [pltpu.make_async_copy(right.at[j], right_all.at[j, :, span_of(i)], own_sem.at[1 + j]) for j in range(bands)]
    for copy in own:
        copy.start()

    @pl.when(i == 0)
    def _():
        near[0, :part] = edge_r[0]

    @pl.when(i == rows - 1)
    def _():
        near[1, (rows - 1) * part :] = edge_r[1]

    @pl.when(c == 0)
    def _():
        edge_all[0] = edge_c[0]

    @pl.when(c == cols - 1)
    def _():
        edge_all[cols - 1] = edge_c[1]

    def pass_z(d, j):
        for way in (1, 0):
            r = i - 2 * d if way else i + 2 * d

            @pl.when((r >= 0) & (r < rows))
            def _():
                r_copy_z(j, d, way, r, piece(j, r)).wait_recv()

                @pl.when(up if way else down)
                def _():
                    r_copy_z(j, d, way, r, piece(j, r)).start()

    def pass_x(d, j):
        for way in (1, 0):
            r = i - 2 * d if way else i + 2 * d

            @pl.when((r >= 0) & (r < rows))
            def _():
                r_copy_p(j, 2 * d - way, r, piece(j, r)).start()

    def side_z(d):
        for kind in (0, 1):
            mine = i if kind == 0 else pair
            for way in (1, 0):
                r = mine - 2 * d if way else mine + 2 * d

                @pl.when((r >= 0) & (r < rows))
                def _():
                    if d:
                        s_copy_z(kind, d, way, r, side_piece(r)).wait_recv()

                    @pl.when(up if way else down)
                    def _():
                        s_copy_z(kind, d, way, r, right.at[last, 2] if kind + d == 0 else side_piece(r)).start()

    def cov_on(k):
        cov_arrive(k).wait_recv()

        @pl.when(has_onward)
        def _():
            far_copy(k).start()

    taken = 0
    for d in range(1, depth):
        pass_z(d, 0)
        pass_x(d, 0)
        if d == 1:
            for j in range(1, bands):
                own_z(j)
        if d < depth - 1 and taken < CHUNKS - 2:
            cov_on(taken)
            taken += 1
    for j in range(1, bands):
        r_copy_p(j, 0, i, own_piece(j)).start()
        if depth > 1:
            pass_z(1, j)
            pass_x(1, j)

    for k in range(taken, CHUNKS):
        cov_on(k)
    ex.wait_recv()

    @pl.when(i != goal)
    def _():
        edge_copy(0, edge_r.at[odd], i).start()
        edge_copy(1, relay, pair).start()

    @pl.when(i == 0)
    def _():
        near[0, part : 2 * part] = relay[...]

    @pl.when(i == rows - 1)
    def _():
        near[1, (rows - 2) * part : (rows - 1) * part] = relay[...]

    s_copy_x(pair).wait_recv()
    side_z(0)
    for copy in own:
        copy.wait()
    for k in range(1, cols):
        source = lax.rem(c + k, cols)
        remote(left.at[0], left_all.at[source], l_send.at[k], l_recv.at[source], col=source).wait_recv()
    width = left_all.shape[3]
    for k in range(cols):
        for m in range(3):
            high, low = halves(left_all[k, m])
            l_high[m, :, k * width : (k + 1) * width] = high
            l_low[m, :, k * width : (k + 1) * width] = low

    per_band = block // TILE

    def left_product(m, source, t):
        high, low = halves(source)
        return product(l_high[m], l_low[m], high, low, False)

    def tile_of(t):
        return t // per_band, pl.ds(pl.multiple_of(lax.rem(t, per_band) * TILE, TILE), TILE)

    @pl.loop(0, bands * per_band)
    def _(t):
        band, span = tile_of(t)
        flat = pl.ds(pl.multiple_of(t * TILE, TILE), TILE)
        half[band, :, span] = left_product(1, cov[:, flat], t)

    for j in range(1, bands):
        if depth > 2:
            pass_z(2, j)
            pass_x(2, j)

    @pl.loop(0, bands * per_band)
    def _(t):
        band, span = tile_of(t)
        flat = pl.ds(pl.multiple_of(t * TILE, TILE), TILE)
        half[band, :, span] += left_product(2 - 2 * odd, near[1 - odd, :, flat], t)

    @pl.when(fed)
    def _():
        for k in range(CHUNKS):
            rng = pl.ds(k * step_rows, step_rows)
            remote(cov.at[rng], near.at[odd, rng], f_send.at[k], f_recv.at[k], row=pair).wait_recv()

    @pl.when(jnp.logical_not(fed))
    def _():
        for k in range(rows - 2):
            edge_copy(0, edge_r.at[0], 2 - 2 * odd + k).wait_recv()

    @pl.loop(0, bands * per_band)
    def _(t):
        band, span = tile_of(t)
        flat = pl.ds(pl.multiple_of(t * TILE, TILE), TILE)
        total = half[band, :, span] + left_product(2 * odd, near[odd, :, flat], t)
        half[band, :, span] = total
        high, low = halves(total)
        w_high[band + 1, :, span] = high
        w_low[band + 1, :, span] = low

    to_right = remote(half.at[bands - 1], halo.at[0], h_send.at[0], h_recv.at[0], col=c + 1)
    to_left = remote(half.at[0], halo.at[1], h_send.at[1], h_recv.at[1], col=c - 1)

    @pl.when(c < cols - 1)
    def _():
        to_right.start()

    @pl.when(c > 0)
    def _():
        to_left.start()

    for d in range(3, depth):
        for j in range(1, bands):
            pass_z(d, j)
            pass_x(d, j)
    if depth > 1:
        side_z(1)

    def store_halo(side, inner, copy):
        at = side * (bands + 1)

        @pl.when(inner)
        def _():
            copy.wait_recv()
            high, low = halves(halo[side])
            w_high[at] = high
            w_low[at] = low

        @pl.when(jnp.logical_not(inner))
        def _():
            for k in range(1, cols):
                source = lax.rem(c + k, cols)
                remote(
                    edge_c.at[0], edge_all.at[source], ec_send.at[0], ec_recv.at[source], col=source
                ).wait_recv()
            for k in range(cols):
                high, low = halves(edge_all[k])
                w_high[at, :, k * width : (k + 1) * width] = high
                w_low[at, :, k * width : (k + 1) * width] = low

    store_halo(0, c > 0, to_right)
    store_halo(1, c < cols - 1, to_left)
    for d in range(2, depth - 1):
        side_z(d)

    for j in range(bands):
        for z in range(depth):
            r = 2 * z + 1 - odd
            r_copy_p(j, 0, r, piece(j, r)).wait_recv()
        if j == last and depth > 2:
            side_z(depth - 1)

        @pl.loop(0, per_band)
        def _(t):
            span = pl.ds(pl.multiple_of(t * TILE, TILE), TILE)
            total = None
            for m in range(3):
                high, low = halves(right_all[j, m, span, :])
                term = product(w_high[j + m], w_low[j + m], high, low, True)
                total = term if total is None else total + term
            out[:, pl.ds(pl.multiple_of(j * block + t * TILE, TILE), TILE)] = total

    for k in range(CHUNKS):
        cov_copy(k).wait_send()

        @pl.when(has_onward)
        def _():
            far_copy(k).wait_send()

    for k in range(1, cols):
        l_copy(k).wait_send()
    for j in range(bands):
        r_copy_p(j, 0, i, own_piece(j)).wait_send()
        for d in range(depth):
            for way in (1, 0):
                r = i - 2 * d if way else i + 2 * d

                @pl.when((r >= 0) & (r < rows))
                def _():
                    @pl.when(up if way else down)
                    def _():
                        r_copy_z(j, d, way, r, piece(j, r)).wait_send()

                    if d:
                        r_copy_p(j, 2 * d - way, r, piece(j, r)).wait_send()

    ex.wait_send()
    s_copy_x(i).wait_send()
    for d in range(depth):
        for kind in (0, 1):
            mine = i if kind == 0 else pair
            for way in (1, 0):
                r = mine - 2 * d if way else mine + 2 * d

                @pl.when((r >= 0) & (r < rows) & (up if way else down))
                def _():
                    s_copy_z(kind, d, way, r, side_piece(r)).wait_send()


    @pl.when(i != goal)
    def _():
        edge_copy(0, edge_r.at[odd], i).wait_send()
        edge_copy(1, relay, pair).wait_send()

    @pl.when(c != 0)
    def _():
        ec0.wait_send()

    @pl.when(c != cols - 1)
    def _():
        ec1.wait_send()

    @pl.when(c < cols - 1)
    def _():
        to_right.wait_send()

    @pl.when(c > 0)
    def _():
        to_left.wait_send()


def solution(mesh):
    rows, cols = mesh.shape["row"], mesh.shape["col"]

    def on_device(covariance, left_ops, right_ops, edge_rows, edge_cols):
        block = covariance.shape[0]
        bands, _, part, _ = right_ops.shape
        width = left_ops.shape[3]
        edge_cols = jnp.transpose(edge_cols, (1, 0, 2))
        dma = pltpu.SemaphoreType.DMA
        depth = rows // 2
        return pl.pallas_call(
            functools.partial(kernel, rows, cols),
            out_shape=jax.ShapeDtypeStruct(covariance.shape, F32),
            in_specs=[pl.BlockSpec(memory_space=pltpu.VMEM)] * 5,
            out_specs=pl.BlockSpec(memory_space=pltpu.VMEM),
            scratch_shapes=[
                pltpu.VMEM((2,) + covariance.shape, F32),
                pltpu.VMEM((cols, 3, block, width), F32),
                pltpu.VMEM((bands, 3, block, block), F32),
                pltpu.VMEM((cols, block, width), F32),
                pltpu.VMEM((bands, block, block), F32),
                pltpu.VMEM((2, block, block), F32),
                pltpu.VMEM((part, covariance.shape[1]), F32),
                pltpu.VMEM((3, block, block), BF16),
                pltpu.VMEM((3, block, block), BF16),
                pltpu.VMEM((bands + 2, block, block), BF16),
                pltpu.VMEM((bands + 2, block, block), BF16),
                dma((CHUNKS,)), dma((CHUNKS,)), dma((CHUNKS,)), dma((CHUNKS,)),
                dma((cols,)), dma((cols,)),
                dma((bands, 2, depth)), dma((bands, 2 * depth)), dma((bands, rows)),
                dma((2,)), dma((rows,)), dma((1,)), dma((1,)), dma((2,)), dma((cols,)), dma((2,)), dma((2,)),
                dma((1,)), dma((2, 2, depth)), dma((rows,)), dma((1 + bands,)),
            ],
            compiler_params=pltpu.CompilerParams(
                collective_id=0, has_side_effects=True, vmem_limit_bytes=63 * 1024 * 1024
            ),
        )(covariance, left_ops, right_ops, edge_rows, edge_cols)

    return jax.shard_map(
        on_device,
        mesh=mesh,
        in_specs=(
            P("row", "col"),
            P("row", None, None, "col"),
            P("col", None, "row", None),
            P(None, "row", "col"),
            P("row", None, "col"),
        ),
        out_specs=P("row", "col"),
        check_vma=False,
    )
```

```python
import functools

import jax
import jax.numpy as jnp
from jax import lax
from jax.experimental import pallas as pl
from jax.experimental.pallas import tpu as pltpu
from jax.sharding import PartitionSpec as P

F32, BF16 = jnp.float32, jnp.bfloat16
TILE = 256
CHUNKS = 4


def halves(value):
    high = value.astype(BF16)
    return high, (value - high.astype(F32)).astype(BF16)


def product(a_high, a_low, b_high, b_low, transposed):
    dims = (((1,), (1 if transposed else 0,)), ((), ()))
    dot = functools.partial(lax.dot_general, dimension_numbers=dims, preferred_element_type=F32)
    return dot(a_high, b_high) + (dot(a_high, b_low) + dot(a_low, b_high))


def kernel(
    rows, cols, cov, left, right, edge_r, edge_c, out,
    cov_here, done,
    near, left_all, right_all, edge_all, half, halo, relay, l_high, l_low, w_high, w_low,
    c_send, c_recv, f_send, f_recv, l_send, l_recv, rz_send, rp_send, r_recv, er_send, er_recv, ex_send, ex_recv,
    ec_send, ec_recv, h_send, h_recv, sx_send, sz_send, s_recv, own_sem, out_sem,
):
    i, c = lax.axis_index("row"), lax.axis_index("col")
    block = cov.shape[0]
    bands = right.shape[0]
    part = right.shape[2]
    depth = rows // 2
    odd = lax.rem(i, 2)
    pair = i + 1 - 2 * odd
    onward = i + 2 - 4 * odd
    has_onward = (onward >= 0) & (onward < rows)
    fed = (i - 2 + 4 * odd >= 0) & (i - 2 + 4 * odd < rows)
    step_rows = block // CHUNKS

    def remote(src, dst, send, recv, row=None, col=None):
        target = (i if row is None else row, c if col is None else col)
        return pltpu.make_async_remote_copy(
            src_ref=src, dst_ref=dst, send_sem=send, recv_sem=recv,
            device_id=target, device_id_type=pl.DeviceIdType.MESH,
        )

    own = [pltpu.make_async_copy(left.at[0], left_all.at[c], own_sem.at[0])]
    own += [
        pltpu.make_async_copy(
            right.at[j],
            right_all.at[j, :, pl.ds(pl.multiple_of(i * part, part), part)],
            own_sem.at[1 + j],
        )
        for j in range(bands)
    ]
    own.append(pltpu.make_async_copy(cov, cov_here, own_sem.at[1 + bands]))
    for copy in own:
        copy.start()

    def side_c(k):
        return edge_c.at[:, k, :]

    edges = (
        (i == 0, edge_r.at[0], near.at[0, :part]),
        (i == rows - 1, edge_r.at[1], near.at[1, (rows - 1) * part :]),
        (c == 0, side_c(0), edge_all.at[0]),
        (c == cols - 1, side_c(1), edge_all.at[cols - 1]),
    )
    for k, (here, src, dst) in enumerate(edges):
        @pl.when(here)
        def _():
            pltpu.make_async_copy(src, dst, own_sem.at[2 + bands + k]).start()

    barrier = pltpu.get_barrier_semaphore()
    for k in range(1, rows):
        pl.semaphore_signal(
            barrier, inc=1, device_id=(lax.rem(i + k, rows), c), device_id_type=pl.DeviceIdType.MESH
        )
    for k in range(1, cols):
        pl.semaphore_signal(
            barrier, inc=1, device_id=(i, lax.rem(c + k, cols)), device_id_type=pl.DeviceIdType.MESH
        )
    pl.semaphore_wait(barrier, rows + cols - 2)

    last = bands - 1

    def span_of(r):
        return pl.ds(pl.multiple_of(r * part, part), part)

    def piece(j, r):
        return right_all.at[j, pl.ds(0, 2 if j == last else 3), span_of(r), :]

    def own_piece(j):
        return right.at[j, pl.ds(0, 2 if j == last else 3)]

    def side_piece(r):
        return right_all.at[last, 2, span_of(r), :]

    def s_copy_z(kind, d, way, r, src):
        return remote(
            src, side_piece(r), sz_send.at[kind, way, d], s_recv.at[r], row=i + (2 if way else -2)
        )

    def s_copy_x(r):
        return remote(right.at[last, 2], side_piece(r), sx_send.at[0], s_recv.at[r], row=pair)

    def cov_copy(k):
        rng = pl.ds(k * step_rows, step_rows)
        return remote(cov.at[rng], near.at[odd, rng], c_send.at[k], c_recv.at[k], row=pair)

    def cov_arrive(k):
        rng = pl.ds(k * step_rows, step_rows)
        return remote(cov.at[rng], near.at[1 - odd, rng], c_send.at[k], c_recv.at[k], row=pair)

    def far_copy(k):
        rng = pl.ds(k * step_rows, step_rows)
        return remote(near.at[1 - odd, rng], near.at[odd, rng], f_send.at[k], f_recv.at[k], row=onward)

    def r_copy_z(j, d, way, r, src):
        return remote(src, piece(j, r), rz_send.at[j, way, d], r_recv.at[j, r], row=i + (2 if way else -2))

    def r_copy_p(j, slot, r, src):
        return remote(src, piece(j, r), rp_send.at[j, slot], r_recv.at[j, r], row=pair)

    for k in range(CHUNKS):
        cov_copy(k).start()
    up, down = i + 2 < rows, i - 2 >= 0

    def own_z(j):
        @pl.when(up)
        def _():
            r_copy_z(j, 0, 1, i, own_piece(j)).start()

        @pl.when(down)
        def _():
            r_copy_z(j, 0, 0, i, own_piece(j)).start()

    own_z(0)
    ex = remote(edge_r.at[1 - odd], relay, ex_send.at[0], ex_recv.at[0], row=pair)
    ex.start()
    r_copy_p(0, 0, i, own_piece(0)).start()
    s_copy_x(i).start()

    def l_copy(k):
        return remote(left.at[0], left_all.at[c], l_send.at[k], l_recv.at[c], col=lax.rem(c + k, cols))

    for k in range(1, cols):
        l_copy(k).start()
    goal = odd * (rows - 1)

    def edge_copy(k, src, r):
        dst = near.at[odd, pl.ds(pl.multiple_of(r * part, part), part)]
        return remote(src, dst, er_send.at[k], er_recv.at[r], row=goal)

    ec0 = remote(side_c(0), edge_all.at[c], ec_send.at[0], ec_recv.at[c], col=0)
    ec1 = remote(side_c(1), edge_all.at[c], ec_send.at[1], ec_recv.at[c], col=cols - 1)

    @pl.when(c != 0)
    def _():
        ec0.start()

    @pl.when(c != cols - 1)
    def _():
        ec1.start()

    def pass_z(d, j):
        for way in (1, 0):
            r = i - 2 * d if way else i + 2 * d

            @pl.when((r >= 0) & (r < rows))
            def _():
                r_copy_z(j, d, way, r, piece(j, r)).wait_recv()

                @pl.when(up if way else down)
                def _():
                    r_copy_z(j, d, way, r, piece(j, r)).start()

    def pass_x(d, j):
        for way in (1, 0):
            r = i - 2 * d if way else i + 2 * d

            @pl.when((r >= 0) & (r < rows))
            def _():
                r_copy_p(j, 2 * d - way, r, piece(j, r)).start()

    def side_z(d):
        for kind in (0, 1):
            mine = i if kind == 0 else pair
            for way in (1, 0):
                r = mine - 2 * d if way else mine + 2 * d

                @pl.when((r >= 0) & (r < rows))
                def _():
                    if d:
                        s_copy_z(kind, d, way, r, side_piece(r)).wait_recv()

                    @pl.when(up if way else down)
                    def _():
                        s_copy_z(kind, d, way, r, right.at[last, 2] if kind + d == 0 else side_piece(r)).start()

    def cov_on(k):
        cov_arrive(k).wait_recv()

        @pl.when(has_onward)
        def _():
            far_copy(k).start()

    taken = 0
    for d in range(1, depth):
        pass_z(d, 0)
        pass_x(d, 0)
        if d == 1:
            for j in range(1, bands):
                own_z(j)
        if d < depth - 1 and taken < CHUNKS - 2:
            cov_on(taken)
            taken += 1
    for j in range(1, bands):
        r_copy_p(j, 0, i, own_piece(j)).start()
        if depth > 1:
            pass_z(1, j)
            pass_x(1, j)

    for k in range(taken, CHUNKS):
        cov_on(k)
    ex.wait_recv()

    @pl.when(i != goal)
    def _():
        edge_copy(0, edge_r.at[odd], i).start()
        edge_copy(1, relay, pair).start()

    @pl.when(i == 0)
    def _():
        near[0, part : 2 * part] = relay[...]

    @pl.when(i == rows - 1)
    def _():
        near[1, (rows - 2) * part : (rows - 1) * part] = relay[...]

    s_copy_x(pair).wait_recv()
    side_z(0)
    for copy in own:
        copy.wait()
    for k, (here, src, dst) in enumerate(edges):
        @pl.when(here)
        def _():
            pltpu.make_async_copy(src, dst, own_sem.at[2 + bands + k]).wait()

    for k in range(1, cols):
        source = lax.rem(c + k, cols)
        remote(left.at[0], left_all.at[source], l_send.at[k], l_recv.at[source], col=source).wait_recv()
    width = left_all.shape[3]
    for k in range(cols):
        for m in range(3):
            high, low = halves(left_all[k, m])
            l_high[m, :, k * width : (k + 1) * width] = high
            l_low[m, :, k * width : (k + 1) * width] = low

    per_band = block // TILE

    def left_product(m, source, t):
        high, low = halves(source)
        return product(l_high[m], l_low[m], high, low, False)

    def tile_of(t):
        return t // per_band, pl.ds(pl.multiple_of(lax.rem(t, per_band) * TILE, TILE), TILE)

    @pl.loop(0, bands * per_band)
    def _(t):
        band, span = tile_of(t)
        flat = pl.ds(pl.multiple_of(t * TILE, TILE), TILE)
        half[band, :, span] = left_product(1, cov_here[:, flat], t)

    for j in range(1, bands):
        if depth > 2:
            pass_z(2, j)
            pass_x(2, j)

    @pl.loop(0, bands * per_band)
    def _(t):
        band, span = tile_of(t)
        flat = pl.ds(pl.multiple_of(t * TILE, TILE), TILE)
        half[band, :, span] += left_product(2 - 2 * odd, near[1 - odd, :, flat], t)

    @pl.when(fed)
    def _():
        for k in range(CHUNKS):
            rng = pl.ds(k * step_rows, step_rows)
            remote(cov.at[rng], near.at[odd, rng], f_send.at[k], f_recv.at[k], row=pair).wait_recv()

    @pl.when(jnp.logical_not(fed))
    def _():
        for k in range(rows - 2):
            edge_copy(0, edge_r.at[0], 2 - 2 * odd + k).wait_recv()

    @pl.loop(0, bands * per_band)
    def _(t):
        band, span = tile_of(t)
        flat = pl.ds(pl.multiple_of(t * TILE, TILE), TILE)
        total = half[band, :, span] + left_product(2 * odd, near[odd, :, flat], t)
        half[band, :, span] = total
        high, low = halves(total)
        w_high[band + 1, :, span] = high
        w_low[band + 1, :, span] = low

    to_right = remote(half.at[bands - 1], halo.at[0], h_send.at[0], h_recv.at[0], col=c + 1)
    to_left = remote(half.at[0], halo.at[1], h_send.at[1], h_recv.at[1], col=c - 1)

    @pl.when(c < cols - 1)
    def _():
        to_right.start()

    @pl.when(c > 0)
    def _():
        to_left.start()

    for d in range(3, depth):
        for j in range(1, bands):
            pass_z(d, j)
            pass_x(d, j)
    if depth > 1:
        side_z(1)

    def store_halo(side, inner, copy):
        at = side * (bands + 1)

        @pl.when(inner)
        def _():
            copy.wait_recv()
            high, low = halves(halo[side])
            w_high[at] = high
            w_low[at] = low

        @pl.when(jnp.logical_not(inner))
        def _():
            for k in range(1, cols):
                source = lax.rem(c + k, cols)
                remote(
                    side_c(0), edge_all.at[source], ec_send.at[0], ec_recv.at[source], col=source
                ).wait_recv()
            for k in range(cols):
                high, low = halves(edge_all[k])
                w_high[at, :, k * width : (k + 1) * width] = high
                w_low[at, :, k * width : (k + 1) * width] = low

    store_halo(0, c > 0, to_right)
    store_halo(1, c < cols - 1, to_left)
    for d in range(2, depth - 1):
        side_z(d)

    per_tile = TILE // part
    late = i >= rows // 2

    def result_copy(j, t):
        flat = pl.ds(pl.multiple_of(j * block + t * TILE, TILE), TILE)
        return pltpu.make_async_copy(
            done.at[:, flat], out.at[:, flat], out_sem.at[j * per_band + t]
        )

    for j in range(bands):
        if j == last and depth > 2:
            side_z(depth - 1)

        @pl.loop(0, per_band)
        def _(step):
            t = jnp.where(late, per_band - 1 - step, step)

            @pl.loop(0, per_tile // 2)
            def _(q):
                r = t * per_tile + 2 * q + 1 - odd
                r_copy_p(j, 0, r, piece(j, r)).wait_recv()

            span = pl.ds(pl.multiple_of(t * TILE, TILE), TILE)
            total = None
            for m in range(3):
                high, low = halves(right_all[j, m, span, :])
                term = product(w_high[j + m], w_low[j + m], high, low, True)
                total = term if total is None else total + term
            done[:, pl.ds(pl.multiple_of(j * block + t * TILE, TILE), TILE)] = total
            result_copy(j, t).start()

    for k in range(CHUNKS):
        cov_copy(k).wait_send()

        @pl.when(has_onward)
        def _():
            far_copy(k).wait_send()

    for k in range(1, cols):
        l_copy(k).wait_send()
    for j in range(bands):
        r_copy_p(j, 0, i, own_piece(j)).wait_send()
        for d in range(depth):
            for way in (1, 0):
                r = i - 2 * d if way else i + 2 * d

                @pl.when((r >= 0) & (r < rows))
                def _():
                    @pl.when(up if way else down)
                    def _():
                        r_copy_z(j, d, way, r, piece(j, r)).wait_send()

                    if d:
                        r_copy_p(j, 2 * d - way, r, piece(j, r)).wait_send()

    for j in range(bands):
        for t in range(per_band):
            result_copy(j, t).wait()
    ex.wait_send()
    s_copy_x(i).wait_send()
    for d in range(depth):
        for kind in (0, 1):
            mine = i if kind == 0 else pair
            for way in (1, 0):
                r = mine - 2 * d if way else mine + 2 * d

                @pl.when((r >= 0) & (r < rows) & (up if way else down))
                def _():
                    s_copy_z(kind, d, way, r, side_piece(r)).wait_send()


    @pl.when(i != goal)
    def _():
        edge_copy(0, edge_r.at[odd], i).wait_send()
        edge_copy(1, relay, pair).wait_send()

    @pl.when(c != 0)
    def _():
        ec0.wait_send()

    @pl.when(c != cols - 1)
    def _():
        ec1.wait_send()

    @pl.when(c < cols - 1)
    def _():
        to_right.wait_send()

    @pl.when(c > 0)
    def _():
        to_left.wait_send()


def solution(mesh):
    rows, cols = mesh.shape["row"], mesh.shape["col"]

    def on_device(covariance, left_ops, right_ops, edge_rows, edge_cols):
        block = covariance.shape[0]
        bands, _, part, _ = right_ops.shape
        width = left_ops.shape[3]
        dma = pltpu.SemaphoreType.DMA
        depth = rows // 2
        return pl.pallas_call(
            functools.partial(kernel, rows, cols),
            out_shape=jax.ShapeDtypeStruct(covariance.shape, F32),
            in_specs=[pl.BlockSpec(memory_space=pl.ANY)] * 5,
            out_specs=pl.BlockSpec(memory_space=pl.ANY),
            scratch_shapes=[
                pltpu.VMEM(covariance.shape, F32),
                pltpu.VMEM(covariance.shape, F32),
                pltpu.VMEM((2,) + covariance.shape, F32),
                pltpu.VMEM((cols, 3, block, width), F32),
                pltpu.VMEM((bands, 3, block, block), F32),
                pltpu.VMEM((cols, block, width), F32),
                pltpu.VMEM((bands, block, block), F32),
                pltpu.VMEM((2, block, block), F32),
                pltpu.VMEM((part, covariance.shape[1]), F32),
                pltpu.VMEM((3, block, block), BF16),
                pltpu.VMEM((3, block, block), BF16),
                pltpu.VMEM((bands + 2, block, block), BF16),
                pltpu.VMEM((bands + 2, block, block), BF16),
                dma((CHUNKS,)), dma((CHUNKS,)), dma((CHUNKS,)), dma((CHUNKS,)),
                dma((cols,)), dma((cols,)),
                dma((bands, 2, depth)), dma((bands, 2 * depth)), dma((bands, rows)),
                dma((2,)), dma((rows,)), dma((1,)), dma((1,)), dma((2,)), dma((cols,)), dma((2,)), dma((2,)),
                dma((1,)), dma((2, 2, depth)), dma((rows,)), dma((6 + bands,)),
                dma((bands * block // TILE,)),
            ],
            compiler_params=pltpu.CompilerParams(
                collective_id=0, has_side_effects=True, vmem_limit_bytes=63 * 1024 * 1024
            ),
        )(covariance, left_ops, right_ops, edge_rows, edge_cols)

    return jax.shard_map(
        on_device,
        mesh=mesh,
        in_specs=(
            P("row", "col"),
            P("row", None, None, "col"),
            P("col", None, "row", None),
            P(None, "row", "col"),
            P("row", None, "col"),
        ),
        out_specs=P("row", "col"),
        check_vma=False,
    )
```

```python
import functools

import jax
import jax.numpy as jnp
from jax import lax
from jax.experimental import pallas as pl
from jax.experimental.pallas import tpu as pltpu
from jax.sharding import PartitionSpec as P

F32, BF16 = jnp.float32, jnp.bfloat16
TILE = 256
CHUNKS = 4


def halves(value):
    high = value.astype(BF16)
    return high, (value - high.astype(F32)).astype(BF16)


def product(a_high, a_low, b_high, b_low, transposed):
    dims = (((1,), (1 if transposed else 0,)), ((), ()))
    dot = functools.partial(lax.dot_general, dimension_numbers=dims, preferred_element_type=F32)
    return dot(a_high, b_high) + (dot(a_high, b_low) + dot(a_low, b_high))


def kernel(
    rows, cols, cov, left, right, edge_r, edge_c, out,
    cov_here, done,
    near, left_all, right_all, edge_all, half, halo, relay, l_high, l_low, w_high, w_low,
    c_send, c_recv, f_send, f_recv, l_send, l_recv, rz_send, rp_send, r_recv, er_send, er_recv, ex_send, ex_recv,
    ec_send, ec_recv, h_send, h_recv, sx_send, sz_send, s_recv, own_sem, out_sem,
):
    i, c = lax.axis_index("row"), lax.axis_index("col")
    block = cov.shape[0]
    bands = right.shape[0]
    part = right.shape[2]
    depth = rows // 2
    odd = lax.rem(i, 2)
    pair = i + 1 - 2 * odd
    onward = i + 2 - 4 * odd
    has_onward = (onward >= 0) & (onward < rows)
    fed = (i - 2 + 4 * odd >= 0) & (i - 2 + 4 * odd < rows)
    step_rows = block // CHUNKS

    def remote(src, dst, send, recv, row=None, col=None):
        target = (i if row is None else row, c if col is None else col)
        return pltpu.make_async_remote_copy(
            src_ref=src, dst_ref=dst, send_sem=send, recv_sem=recv,
            device_id=target, device_id_type=pl.DeviceIdType.MESH,
        )

    own = [pltpu.make_async_copy(left.at[0], left_all.at[c], own_sem.at[0])]
    own += [
        pltpu.make_async_copy(
            right.at[j],
            right_all.at[j, :, pl.ds(pl.multiple_of(i * part, part), part)],
            own_sem.at[1 + j],
        )
        for j in range(bands)
    ]
    own.append(pltpu.make_async_copy(cov, cov_here, own_sem.at[1 + bands]))
    for copy in own:
        copy.start()

    def side_c(k):
        return edge_c.at[:, k, :]

    edges = (
        (i == 0, edge_r.at[0], near.at[0, :part]),
        (i == rows - 1, edge_r.at[1], near.at[1, (rows - 1) * part :]),
        (c == 0, side_c(0), edge_all.at[0]),
        (c == cols - 1, side_c(1), edge_all.at[cols - 1]),
    )
    for k, (here, src, dst) in enumerate(edges):
        @pl.when(here)
        def _():
            pltpu.make_async_copy(src, dst, own_sem.at[2 + bands + k]).start()

    barrier = pltpu.get_barrier_semaphore()
    for k in range(1, rows):
        pl.semaphore_signal(
            barrier, inc=1, device_id=(lax.rem(i + k, rows), c), device_id_type=pl.DeviceIdType.MESH
        )
    for k in range(1, cols):
        pl.semaphore_signal(
            barrier, inc=1, device_id=(i, lax.rem(c + k, cols)), device_id_type=pl.DeviceIdType.MESH
        )
    pl.semaphore_wait(barrier, rows + cols - 2)

    last = bands - 1
    units = [(j, pl.ds(0, 3)) for j in range(last)] + [(last, pl.ds(0, 1)), (last, pl.ds(1, 1))]
    count = len(units)

    def span_of(r):
        return pl.ds(pl.multiple_of(r * part, part), part)

    def piece(j, r):
        return right_all.at[units[j][0], units[j][1], span_of(r), :]

    def own_piece(j):
        return right.at[units[j][0], units[j][1]]

    def at_end(r):
        return (r < 2) | (r >= rows - 2)

    def goes(j, r):
        return jnp.logical_not(at_end(r)) if j == len(units) - 1 else r >= 0

    def side_piece(r, q):
        return right_all.at[last, 2 - q, span_of(r), :]

    def s_copy_z(kind, d, way, r, src, q):
        return remote(
            src, side_piece(r, q), sz_send.at[q, kind, way, d], s_recv.at[q, r],
            row=i + (2 if way else -2),
        )

    def s_copy_x(r, q):
        return remote(right.at[last, 2 - q], side_piece(r, q), sx_send.at[q], s_recv.at[q, r], row=pair)

    def cov_copy(k):
        rng = pl.ds(k * step_rows, step_rows)
        return remote(cov.at[rng], near.at[odd, rng], c_send.at[k], c_recv.at[k], row=pair)

    def cov_arrive(k):
        rng = pl.ds(k * step_rows, step_rows)
        return remote(cov.at[rng], near.at[1 - odd, rng], c_send.at[k], c_recv.at[k], row=pair)

    def far_copy(k):
        rng = pl.ds(k * step_rows, step_rows)
        return remote(near.at[1 - odd, rng], near.at[odd, rng], f_send.at[k], f_recv.at[k], row=onward)

    def r_copy_z(j, d, way, r, src):
        return remote(src, piece(j, r), rz_send.at[j, way, d], r_recv.at[j, r], row=i + (2 if way else -2))

    def r_copy_p(j, slot, r, src):
        return remote(src, piece(j, r), rp_send.at[j, slot], r_recv.at[j, r], row=pair)

    for k in range(CHUNKS):
        cov_copy(k).start()
    up, down = i + 2 < rows, i - 2 >= 0

    def own_z(j):
        @pl.when(up & goes(j, i))
        def _():
            r_copy_z(j, 0, 1, i, own_piece(j)).start()

        @pl.when(down & goes(j, i))
        def _():
            r_copy_z(j, 0, 0, i, own_piece(j)).start()

    own_z(0)
    ex = remote(edge_r.at[1 - odd], relay, ex_send.at[0], ex_recv.at[0], row=pair)
    ex.start()
    r_copy_p(0, 0, i, own_piece(0)).start()
    s_copy_x(i, 0).start()

    @pl.when(at_end(i))
    def _():
        s_copy_x(i, 1).start()

    def l_copy(k):
        return remote(left.at[0], left_all.at[c], l_send.at[k], l_recv.at[c], col=lax.rem(c + k, cols))

    for k in range(1, cols):
        l_copy(k).start()
    goal = odd * (rows - 1)

    def edge_copy(k, src, r):
        dst = near.at[odd, pl.ds(pl.multiple_of(r * part, part), part)]
        return remote(src, dst, er_send.at[k], er_recv.at[r], row=goal)

    ec0 = remote(side_c(0), edge_all.at[c], ec_send.at[0], ec_recv.at[c], col=0)
    ec1 = remote(side_c(1), edge_all.at[c], ec_send.at[1], ec_recv.at[c], col=cols - 1)

    @pl.when(c != 0)
    def _():
        ec0.start()

    @pl.when(c != cols - 1)
    def _():
        ec1.start()

    def pass_z(d, j):
        for way in (1, 0):
            r = i - 2 * d if way else i + 2 * d

            @pl.when((r >= 0) & (r < rows) & goes(j, r))
            def _():
                r_copy_z(j, d, way, r, piece(j, r)).wait_recv()

                @pl.when(up if way else down)
                def _():
                    r_copy_z(j, d, way, r, piece(j, r)).start()

    def pass_x(d, j):
        for way in (1, 0):
            r = i - 2 * d if way else i + 2 * d

            @pl.when((r >= 0) & (r < rows) & goes(j, r))
            def _():
                r_copy_p(j, 2 * d - way, r, piece(j, r)).start()

    def side_z(d):
        for q in (0, 1):
            for kind in (0, 1):
                mine = i if kind == 0 else pair
                for way in (1, 0):
                    r = mine - 2 * d if way else mine + 2 * d

                    @pl.when((r >= 0) & (r < rows) & (at_end(r) if q else r >= 0))
                    def _():
                        if d:
                            s_copy_z(kind, d, way, r, side_piece(r, q), q).wait_recv()

                        @pl.when(up if way else down)
                        def _():
                            src = right.at[last, 2 - q] if kind + d == 0 else side_piece(r, q)
                            s_copy_z(kind, d, way, r, src, q).start()

    def cov_on(k):
        cov_arrive(k).wait_recv()

        @pl.when(has_onward)
        def _():
            far_copy(k).start()

    taken = 0
    for d in range(1, depth):
        pass_z(d, 0)
        pass_x(d, 0)
        if d == 1:
            for j in range(1, count):
                own_z(j)
        if d < depth - 1 and taken < CHUNKS - 2:
            cov_on(taken)
            taken += 1
    for j in range(1, count):
        @pl.when(goes(j, i))
        def _():
            r_copy_p(j, 0, i, own_piece(j)).start()

        if depth > 1:
            pass_z(1, j)
            pass_x(1, j)

    for k in range(taken, CHUNKS):
        cov_on(k)
    ex.wait_recv()

    @pl.when(i != goal)
    def _():
        edge_copy(0, edge_r.at[odd], i).start()
        edge_copy(1, relay, pair).start()

    @pl.when(i == 0)
    def _():
        near[0, part : 2 * part] = relay[...]

    @pl.when(i == rows - 1)
    def _():
        near[1, (rows - 2) * part : (rows - 1) * part] = relay[...]

    s_copy_x(pair, 0).wait_recv()

    @pl.when(at_end(i))
    def _():
        s_copy_x(pair, 1).wait_recv()

    side_z(0)
    for copy in own:
        copy.wait()
    for k, (here, src, dst) in enumerate(edges):
        @pl.when(here)
        def _():
            pltpu.make_async_copy(src, dst, own_sem.at[2 + bands + k]).wait()

    for k in range(1, cols):
        source = lax.rem(c + k, cols)
        remote(left.at[0], left_all.at[source], l_send.at[k], l_recv.at[source], col=source).wait_recv()
    width = left_all.shape[3]
    for k in range(cols):
        for m in range(3):
            high, low = halves(left_all[k, m])
            l_high[m, :, k * width : (k + 1) * width] = high
            l_low[m, :, k * width : (k + 1) * width] = low

    per_band = block // TILE

    def left_product(m, source, t):
        high, low = halves(source)
        return product(l_high[m], l_low[m], high, low, False)

    def tile_of(t):
        return t // per_band, pl.ds(pl.multiple_of(lax.rem(t, per_band) * TILE, TILE), TILE)

    @pl.loop(0, bands * per_band)
    def _(t):
        band, span = tile_of(t)
        flat = pl.ds(pl.multiple_of(t * TILE, TILE), TILE)
        half[band, :, span] = left_product(1, cov_here[:, flat], t)

    for j in range(1, count):
        if depth > 2:
            pass_z(2, j)
            pass_x(2, j)

    @pl.loop(0, bands * per_band)
    def _(t):
        band, span = tile_of(t)
        flat = pl.ds(pl.multiple_of(t * TILE, TILE), TILE)
        half[band, :, span] += left_product(2 - 2 * odd, near[1 - odd, :, flat], t)

    @pl.when(fed)
    def _():
        for k in range(CHUNKS):
            rng = pl.ds(k * step_rows, step_rows)
            remote(cov.at[rng], near.at[odd, rng], f_send.at[k], f_recv.at[k], row=pair).wait_recv()

    @pl.when(jnp.logical_not(fed))
    def _():
        for k in range(rows - 2):
            edge_copy(0, edge_r.at[0], 2 - 2 * odd + k).wait_recv()

    @pl.loop(0, bands * per_band)
    def _(t):
        band, span = tile_of(t)
        flat = pl.ds(pl.multiple_of(t * TILE, TILE), TILE)
        total = half[band, :, span] + left_product(2 * odd, near[odd, :, flat], t)
        half[band, :, span] = total
        high, low = halves(total)
        w_high[band + 1, :, span] = high
        w_low[band + 1, :, span] = low

    to_right = remote(half.at[bands - 1], halo.at[0], h_send.at[0], h_recv.at[0], col=c + 1)
    to_left = remote(half.at[0], halo.at[1], h_send.at[1], h_recv.at[1], col=c - 1)

    @pl.when(c < cols - 1)
    def _():
        to_right.start()

    @pl.when(c > 0)
    def _():
        to_left.start()

    for d in range(3, depth):
        for j in range(1, count):
            pass_z(d, j)
            pass_x(d, j)
    if depth > 1:
        side_z(1)

    def store_halo(side, inner, copy):
        at = side * (bands + 1)

        @pl.when(inner)
        def _():
            copy.wait_recv()
            high, low = halves(halo[side])
            w_high[at] = high
            w_low[at] = low

        @pl.when(jnp.logical_not(inner))
        def _():
            for k in range(1, cols):
                source = lax.rem(c + k, cols)
                remote(
                    side_c(0), edge_all.at[source], ec_send.at[0], ec_recv.at[source], col=source
                ).wait_recv()
            for k in range(cols):
                high, low = halves(edge_all[k])
                w_high[at, :, k * width : (k + 1) * width] = high
                w_low[at, :, k * width : (k + 1) * width] = low

    store_halo(0, c > 0, to_right)
    store_halo(1, c < cols - 1, to_left)
    for d in range(2, depth - 1):
        side_z(d)

    per_tile = TILE // part
    late = i >= rows // 2

    def result_copy(j, t):
        flat = pl.ds(pl.multiple_of(j * block + t * TILE, TILE), TILE)
        return pltpu.make_async_copy(
            done.at[:, flat], out.at[:, flat], out_sem.at[j * per_band + t]
        )

    for j in range(bands):
        if j == last and depth > 2:
            side_z(depth - 1)

        @pl.loop(0, per_band)
        def _(step):
            t = jnp.where(late, per_band - 1 - step, step)

            @pl.loop(0, per_tile // 2)
            def _(q):
                r = t * per_tile + 2 * q + 1 - odd
                for u in range(count):
                    if units[u][0] == j:
                        @pl.when(goes(u, r))
                        def _():
                            r_copy_p(u, 0, r, piece(u, r)).wait_recv()

            span = pl.ds(pl.multiple_of(t * TILE, TILE), TILE)
            total = None
            for m in range(3):
                high, low = halves(right_all[j, m, span, :])
                term = product(w_high[j + m], w_low[j + m], high, low, True)
                total = term if total is None else total + term
            done[:, pl.ds(pl.multiple_of(j * block + t * TILE, TILE), TILE)] = total
            result_copy(j, t).start()

    for k in range(CHUNKS):
        cov_copy(k).wait_send()

        @pl.when(has_onward)
        def _():
            far_copy(k).wait_send()

    for k in range(1, cols):
        l_copy(k).wait_send()
    for j in range(count):
        @pl.when(goes(j, i))
        def _():
            r_copy_p(j, 0, i, own_piece(j)).wait_send()

        for d in range(depth):
            for way in (1, 0):
                r = i - 2 * d if way else i + 2 * d

                @pl.when((r >= 0) & (r < rows) & goes(j, r))
                def _():
                    @pl.when(up if way else down)
                    def _():
                        r_copy_z(j, d, way, r, piece(j, r)).wait_send()

                    if d:
                        r_copy_p(j, 2 * d - way, r, piece(j, r)).wait_send()

    for j in range(bands):
        for t in range(per_band):
            result_copy(j, t).wait()
    ex.wait_send()
    s_copy_x(i, 0).wait_send()

    @pl.when(at_end(i))
    def _():
        s_copy_x(i, 1).wait_send()

    for q in (0, 1):
        for d in range(depth):
            for kind in (0, 1):
                mine = i if kind == 0 else pair
                for way in (1, 0):
                    r = mine - 2 * d if way else mine + 2 * d
                    sent = (r >= 0) & (r < rows) & (up if way else down)

                    @pl.when(sent & at_end(r) if q else sent)
                    def _():
                        s_copy_z(kind, d, way, r, side_piece(r, q), q).wait_send()

    @pl.when(i != goal)
    def _():
        edge_copy(0, edge_r.at[odd], i).wait_send()
        edge_copy(1, relay, pair).wait_send()

    @pl.when(c != 0)
    def _():
        ec0.wait_send()

    @pl.when(c != cols - 1)
    def _():
        ec1.wait_send()

    @pl.when(c < cols - 1)
    def _():
        to_right.wait_send()

    @pl.when(c > 0)
    def _():
        to_left.wait_send()


def solution(mesh):
    rows, cols = mesh.shape["row"], mesh.shape["col"]

    def on_device(covariance, left_ops, right_ops, edge_rows, edge_cols):
        block = covariance.shape[0]
        bands, _, part, _ = right_ops.shape
        width = left_ops.shape[3]
        dma = pltpu.SemaphoreType.DMA
        depth = rows // 2
        return pl.pallas_call(
            functools.partial(kernel, rows, cols),
            out_shape=jax.ShapeDtypeStruct(covariance.shape, F32),
            in_specs=[pl.BlockSpec(memory_space=pl.ANY)] * 5,
            out_specs=pl.BlockSpec(memory_space=pl.ANY),
            scratch_shapes=[
                pltpu.VMEM(covariance.shape, F32),
                pltpu.VMEM(covariance.shape, F32),
                pltpu.VMEM((2,) + covariance.shape, F32),
                pltpu.VMEM((cols, 3, block, width), F32),
                pltpu.VMEM((bands, 3, block, block), F32),
                pltpu.VMEM((cols, block, width), F32),
                pltpu.VMEM((bands, block, block), F32),
                pltpu.VMEM((2, block, block), F32),
                pltpu.VMEM((part, covariance.shape[1]), F32),
                pltpu.VMEM((3, block, block), BF16),
                pltpu.VMEM((3, block, block), BF16),
                pltpu.VMEM((bands + 2, block, block), BF16),
                pltpu.VMEM((bands + 2, block, block), BF16),
                dma((CHUNKS,)), dma((CHUNKS,)), dma((CHUNKS,)), dma((CHUNKS,)),
                dma((cols,)), dma((cols,)),
                dma((bands + 1, 2, depth)), dma((bands + 1, 2 * depth)), dma((bands + 1, rows)),
                dma((2,)), dma((rows,)), dma((1,)), dma((1,)), dma((2,)), dma((cols,)), dma((2,)), dma((2,)),
                dma((2,)), dma((2, 2, 2, depth)), dma((2, rows)), dma((6 + bands,)),
                dma((bands * block // TILE,)),
            ],
            compiler_params=pltpu.CompilerParams(
                collective_id=0, has_side_effects=True, vmem_limit_bytes=63 * 1024 * 1024
            ),
        )(covariance, left_ops, right_ops, edge_rows, edge_cols)

    return jax.shard_map(
        on_device,
        mesh=mesh,
        in_specs=(
            P("row", "col"),
            P("row", None, None, "col"),
            P("col", None, "row", None),
            P(None, "row", "col"),
            P("row", None, "col"),
        ),
        out_specs=P("row", "col"),
        check_vma=False,
    )
```

```python
import functools

import jax
import jax.numpy as jnp
from jax import lax
from jax.experimental import pallas as pl
from jax.experimental.pallas import tpu as pltpu
from jax.sharding import PartitionSpec as P

F32, BF16 = jnp.float32, jnp.bfloat16
TILE = 256
CHUNKS = 4


def halves(value):
    high = value.astype(BF16)
    return high, (value - high.astype(F32)).astype(BF16)


def product(a_high, a_low, b_high, b_low, transposed):
    dims = (((1,), (1 if transposed else 0,)), ((), ()))
    dot = functools.partial(lax.dot_general, dimension_numbers=dims, preferred_element_type=F32)
    return dot(a_high, b_high) + (dot(a_high, b_low) + dot(a_low, b_high))


def kernel(
    rows, cols, cov, left, right, edge_r, edge_c, out,
    cov_here, done,
    near, left_all, right_all, edge_all, half, halo, relay, l_high, l_low, w_high, w_low,
    c_send, c_recv, f_send, f_recv, l_send, l_recv, rz_send, rp_send, r_recv, er_send, er_recv, ex_send, ex_recv,
    ec_send, ec_recv, h_send, h_recv, sx_send, sz_send, s_recv, own_sem, out_sem,
):
    i, c = lax.axis_index("row"), lax.axis_index("col")
    block = cov.shape[0]
    bands = right.shape[0]
    part = right.shape[2]
    depth = rows // 2
    odd = lax.rem(i, 2)
    pair = i + 1 - 2 * odd
    onward = i + 2 - 4 * odd
    has_onward = (onward >= 0) & (onward < rows)
    fed = (i - 2 + 4 * odd >= 0) & (i - 2 + 4 * odd < rows)
    step_rows = block // CHUNKS

    def remote(src, dst, send, recv, row=None, col=None):
        target = (i if row is None else row, c if col is None else col)
        return pltpu.make_async_remote_copy(
            src_ref=src, dst_ref=dst, send_sem=send, recv_sem=recv,
            device_id=target, device_id_type=pl.DeviceIdType.MESH,
        )

    own = [pltpu.make_async_copy(left.at[0], left_all.at[c], own_sem.at[0])]
    own += [
        pltpu.make_async_copy(
            right.at[j],
            right_all.at[j, :, pl.ds(pl.multiple_of(i * part, part), part)],
            own_sem.at[1 + j],
        )
        for j in range(bands)
    ]
    own.append(pltpu.make_async_copy(cov, cov_here, own_sem.at[1 + bands]))
    for copy in own:
        copy.start()

    def side_c(k):
        return edge_c.at[:, k, :]

    edges = (
        (i == 0, edge_r.at[0], near.at[0, :part]),
        (i == rows - 1, edge_r.at[1], near.at[1, (rows - 1) * part :]),
        (c == 0, side_c(0), edge_all.at[0]),
        (c == cols - 1, side_c(1), edge_all.at[cols - 1]),
    )
    for k, (here, src, dst) in enumerate(edges):
        @pl.when(here)
        def _():
            pltpu.make_async_copy(src, dst, own_sem.at[2 + bands + k]).start()

    barrier = pltpu.get_barrier_semaphore()
    for k in range(1, rows):
        pl.semaphore_signal(
            barrier, inc=1, device_id=(lax.rem(i + k, rows), c), device_id_type=pl.DeviceIdType.MESH
        )
    for k in range(1, cols):
        pl.semaphore_signal(
            barrier, inc=1, device_id=(i, lax.rem(c + k, cols)), device_id_type=pl.DeviceIdType.MESH
        )
    pl.semaphore_wait(barrier, rows + cols - 2)

    last = bands - 1
    units = [(j, pl.ds(0, 3)) for j in range(last)] + [(last, pl.ds(0, 1)), (last, pl.ds(1, 1))]
    count = len(units)

    def span_of(r):
        return pl.ds(pl.multiple_of(r * part, part), part)

    def piece(j, r):
        return right_all.at[units[j][0], units[j][1], span_of(r), :]

    def own_piece(j):
        return right.at[units[j][0], units[j][1]]

    def at_end(r):
        return (r < 2) | (r >= rows - 2)

    def goes(j, r):
        return jnp.logical_not(at_end(r)) if j == len(units) - 1 else r >= 0

    def side_piece(r, q):
        return right_all.at[last, 2 - q, span_of(r), :]

    def s_copy_z(kind, d, way, r, src, q):
        return remote(
            src, side_piece(r, q), sz_send.at[q, kind, way, d], s_recv.at[q, r],
            row=i + (2 if way else -2),
        )

    def s_copy_x(r, q):
        return remote(right.at[last, 2 - q], side_piece(r, q), sx_send.at[q], s_recv.at[q, r], row=pair)

    def cov_copy(k):
        rng = pl.ds(k * step_rows, step_rows)
        return remote(cov.at[rng], near.at[odd, rng], c_send.at[k], c_recv.at[k], row=pair)

    def cov_arrive(k):
        rng = pl.ds(k * step_rows, step_rows)
        return remote(cov.at[rng], near.at[1 - odd, rng], c_send.at[k], c_recv.at[k], row=pair)

    def far_copy(k):
        rng = pl.ds(k * step_rows, step_rows)
        return remote(near.at[1 - odd, rng], near.at[odd, rng], f_send.at[k], f_recv.at[k], row=onward)

    def r_copy_z(j, d, way, r, src):
        return remote(src, piece(j, r), rz_send.at[j, way, d], r_recv.at[j, r], row=i + (2 if way else -2))

    def r_copy_p(j, slot, r, src):
        return remote(src, piece(j, r), rp_send.at[j, slot], r_recv.at[j, r], row=pair)

    for k in range(CHUNKS):
        cov_copy(k).start()
    up, down = i + 2 < rows, i - 2 >= 0

    def own_z(j):
        @pl.when(up & goes(j, i))
        def _():
            r_copy_z(j, 0, 1, i, own_piece(j)).start()

        @pl.when(down & goes(j, i))
        def _():
            r_copy_z(j, 0, 0, i, own_piece(j)).start()

    own_z(0)
    ex = remote(edge_r.at[1 - odd], relay, ex_send.at[0], ex_recv.at[0], row=pair)
    ex.start()
    r_copy_p(0, 0, i, own_piece(0)).start()
    s_copy_x(i, 0).start()

    @pl.when(at_end(i))
    def _():
        s_copy_x(i, 1).start()

    def l_copy(k):
        return remote(left.at[0], left_all.at[c], l_send.at[k], l_recv.at[c], col=lax.rem(c + k, cols))

    for k in range(1, cols):
        l_copy(k).start()
    goal = odd * (rows - 1)

    def edge_copy(k, src, r):
        dst = near.at[odd, pl.ds(pl.multiple_of(r * part, part), part)]
        return remote(src, dst, er_send.at[k], er_recv.at[r], row=goal)

    ec0 = remote(side_c(0), edge_all.at[c], ec_send.at[0], ec_recv.at[c], col=0)
    ec1 = remote(side_c(1), edge_all.at[c], ec_send.at[1], ec_recv.at[c], col=cols - 1)

    @pl.when(c != 0)
    def _():
        ec0.start()

    @pl.when(c != cols - 1)
    def _():
        ec1.start()

    def pass_z(d, j):
        for way in (1, 0):
            r = i - 2 * d if way else i + 2 * d

            @pl.when((r >= 0) & (r < rows) & goes(j, r))
            def _():
                r_copy_z(j, d, way, r, piece(j, r)).wait_recv()

                @pl.when(up if way else down)
                def _():
                    r_copy_z(j, d, way, r, piece(j, r)).start()

    def pass_x(d, j):
        for way in (1, 0):
            r = i - 2 * d if way else i + 2 * d

            @pl.when((r >= 0) & (r < rows) & goes(j, r))
            def _():
                r_copy_p(j, 2 * d - way, r, piece(j, r)).start()

    def side_z(d):
        for q in (0, 1):
            for kind in (0, 1):
                mine = i if kind == 0 else pair
                for way in (1, 0):
                    r = mine - 2 * d if way else mine + 2 * d

                    @pl.when((r >= 0) & (r < rows) & (at_end(r) if q else r >= 0))
                    def _():
                        if d:
                            s_copy_z(kind, d, way, r, side_piece(r, q), q).wait_recv()

                        @pl.when(up if way else down)
                        def _():
                            src = right.at[last, 2 - q] if kind + d == 0 else side_piece(r, q)
                            s_copy_z(kind, d, way, r, src, q).start()

    def cov_on(k):
        cov_arrive(k).wait_recv()

        @pl.when(has_onward)
        def _():
            far_copy(k).start()

    taken = 0
    for d in range(1, depth):
        pass_z(d, 0)
        pass_x(d, 0)
        if d == 1:
            for j in range(1, count):
                own_z(j)
        if d < depth - 1 and taken < CHUNKS - 2:
            cov_on(taken)
            taken += 1
    for j in range(1, count):
        @pl.when(goes(j, i))
        def _():
            r_copy_p(j, 0, i, own_piece(j)).start()

        if depth > 1:
            pass_z(1, j)
            pass_x(1, j)

    for k in range(taken, CHUNKS):
        cov_on(k)
    ex.wait_recv()

    @pl.when(i != goal)
    def _():
        edge_copy(0, edge_r.at[odd], i).start()
        edge_copy(1, relay, pair).start()

    @pl.when(i == 0)
    def _():
        near[0, part : 2 * part] = relay[...]

    @pl.when(i == rows - 1)
    def _():
        near[1, (rows - 2) * part : (rows - 1) * part] = relay[...]

    s_copy_x(pair, 0).wait_recv()

    @pl.when(at_end(i))
    def _():
        s_copy_x(pair, 1).wait_recv()

    side_z(0)
    for copy in own:
        copy.wait()
    for k, (here, src, dst) in enumerate(edges):
        @pl.when(here)
        def _():
            pltpu.make_async_copy(src, dst, own_sem.at[2 + bands + k]).wait()

    for k in range(1, cols):
        source = lax.rem(c + k, cols)
        remote(left.at[0], left_all.at[source], l_send.at[k], l_recv.at[source], col=source).wait_recv()
    width = left_all.shape[3]
    for k in range(cols):
        for m in range(3):
            high, low = halves(left_all[k, m])
            l_high[m, :, k * width : (k + 1) * width] = high
            l_low[m, :, k * width : (k + 1) * width] = low

    per_band = block // TILE

    def left_product(m, source, t):
        high, low = halves(source)
        return product(l_high[m], l_low[m], high, low, False)

    def tile_of(t):
        return t // per_band, pl.ds(pl.multiple_of(lax.rem(t, per_band) * TILE, TILE), TILE)

    @pl.loop(0, bands * per_band)
    def _(t):
        band, span = tile_of(t)
        flat = pl.ds(pl.multiple_of(t * TILE, TILE), TILE)
        half[band, :, span] = left_product(1, cov_here[:, flat], t)

    for j in range(1, count):
        if depth > 2:
            pass_z(2, j)
            pass_x(2, j)

    @pl.loop(0, bands * per_band)
    def _(t):
        band, span = tile_of(t)
        flat = pl.ds(pl.multiple_of(t * TILE, TILE), TILE)
        half[band, :, span] += left_product(2 - 2 * odd, near[1 - odd, :, flat], t)

    @pl.when(fed)
    def _():
        for k in range(CHUNKS):
            rng = pl.ds(k * step_rows, step_rows)
            remote(cov.at[rng], near.at[odd, rng], f_send.at[k], f_recv.at[k], row=pair).wait_recv()

    @pl.when(jnp.logical_not(fed))
    def _():
        for k in range(rows - 2):
            edge_copy(0, edge_r.at[0], 2 - 2 * odd + k).wait_recv()

    @pl.loop(0, bands * per_band)
    def _(t):
        band, span = tile_of(t)
        flat = pl.ds(pl.multiple_of(t * TILE, TILE), TILE)
        total = half[band, :, span] + left_product(2 * odd, near[odd, :, flat], t)
        half[band, :, span] = total
        high, low = halves(total)
        w_high[band + 1, :, span] = high
        w_low[band + 1, :, span] = low

    to_right = remote(half.at[bands - 1], halo.at[0], h_send.at[0], h_recv.at[0], col=c + 1)
    to_left = remote(half.at[0], halo.at[1], h_send.at[1], h_recv.at[1], col=c - 1)

    @pl.when(c < cols - 1)
    def _():
        to_right.start()

    @pl.when(c > 0)
    def _():
        to_left.start()

    if depth > 1:
        side_z(1)
    for d in range(3, depth):
        for j in range(1, count):
            pass_z(d, j)
            pass_x(d, j)

    for d in range(2, depth - 1):
        side_z(d)

    def store_halo(side, inner, copy):
        at = side * (bands + 1)

        @pl.when(inner)
        def _():
            copy.wait_recv()
            high, low = halves(halo[side])
            w_high[at] = high
            w_low[at] = low

        @pl.when(jnp.logical_not(inner))
        def _():
            for k in range(1, cols):
                source = lax.rem(c + k, cols)
                remote(
                    side_c(0), edge_all.at[source], ec_send.at[0], ec_recv.at[source], col=source
                ).wait_recv()
            for k in range(cols):
                high, low = halves(edge_all[k])
                w_high[at, :, k * width : (k + 1) * width] = high
                w_low[at, :, k * width : (k + 1) * width] = low

    store_halo(0, c > 0, to_right)
    store_halo(1, c < cols - 1, to_left)

    per_tile = TILE // part
    late = i >= rows // 2

    def result_copy(j, t):
        flat = pl.ds(pl.multiple_of(j * block + t * TILE, TILE), TILE)
        return pltpu.make_async_copy(
            done.at[:, flat], out.at[:, flat], out_sem.at[j * per_band + t]
        )

    for j in range(bands):
        if j == last and depth > 2:
            side_z(depth - 1)

        @pl.loop(0, per_band)
        def _(step):
            t = jnp.where(late, per_band - 1 - step, step)

            @pl.loop(0, per_tile // 2)
            def _(q):
                r = t * per_tile + 2 * q + 1 - odd
                for u in range(count):
                    if units[u][0] == j:
                        @pl.when(goes(u, r))
                        def _():
                            r_copy_p(u, 0, r, piece(u, r)).wait_recv()

            span = pl.ds(pl.multiple_of(t * TILE, TILE), TILE)
            total = None
            for m in range(3):
                high, low = halves(right_all[j, m, span, :])
                term = product(w_high[j + m], w_low[j + m], high, low, True)
                total = term if total is None else total + term
            done[:, pl.ds(pl.multiple_of(j * block + t * TILE, TILE), TILE)] = total
            result_copy(j, t).start()

    for k in range(CHUNKS):
        cov_copy(k).wait_send()

        @pl.when(has_onward)
        def _():
            far_copy(k).wait_send()

    for k in range(1, cols):
        l_copy(k).wait_send()
    for j in range(count):
        @pl.when(goes(j, i))
        def _():
            r_copy_p(j, 0, i, own_piece(j)).wait_send()

        for d in range(depth):
            for way in (1, 0):
                r = i - 2 * d if way else i + 2 * d

                @pl.when((r >= 0) & (r < rows) & goes(j, r))
                def _():
                    @pl.when(up if way else down)
                    def _():
                        r_copy_z(j, d, way, r, piece(j, r)).wait_send()

                    if d:
                        r_copy_p(j, 2 * d - way, r, piece(j, r)).wait_send()

    for j in range(bands):
        for t in range(per_band):
            result_copy(j, t).wait()
    ex.wait_send()
    s_copy_x(i, 0).wait_send()

    @pl.when(at_end(i))
    def _():
        s_copy_x(i, 1).wait_send()

    for q in (0, 1):
        for d in range(depth):
            for kind in (0, 1):
                mine = i if kind == 0 else pair
                for way in (1, 0):
                    r = mine - 2 * d if way else mine + 2 * d
                    sent = (r >= 0) & (r < rows) & (up if way else down)

                    @pl.when(sent & at_end(r) if q else sent)
                    def _():
                        s_copy_z(kind, d, way, r, side_piece(r, q), q).wait_send()

    @pl.when(i != goal)
    def _():
        edge_copy(0, edge_r.at[odd], i).wait_send()
        edge_copy(1, relay, pair).wait_send()

    @pl.when(c != 0)
    def _():
        ec0.wait_send()

    @pl.when(c != cols - 1)
    def _():
        ec1.wait_send()

    @pl.when(c < cols - 1)
    def _():
        to_right.wait_send()

    @pl.when(c > 0)
    def _():
        to_left.wait_send()


def solution(mesh):
    rows, cols = mesh.shape["row"], mesh.shape["col"]

    def on_device(covariance, left_ops, right_ops, edge_rows, edge_cols):
        block = covariance.shape[0]
        bands, _, part, _ = right_ops.shape
        width = left_ops.shape[3]
        dma = pltpu.SemaphoreType.DMA
        depth = rows // 2
        return pl.pallas_call(
            functools.partial(kernel, rows, cols),
            out_shape=jax.ShapeDtypeStruct(covariance.shape, F32),
            in_specs=[pl.BlockSpec(memory_space=pl.ANY)] * 5,
            out_specs=pl.BlockSpec(memory_space=pl.ANY),
            scratch_shapes=[
                pltpu.VMEM(covariance.shape, F32),
                pltpu.VMEM(covariance.shape, F32),
                pltpu.VMEM((2,) + covariance.shape, F32),
                pltpu.VMEM((cols, 3, block, width), F32),
                pltpu.VMEM((bands, 3, block, block), F32),
                pltpu.VMEM((cols, block, width), F32),
                pltpu.VMEM((bands, block, block), F32),
                pltpu.VMEM((2, block, block), F32),
                pltpu.VMEM((part, covariance.shape[1]), F32),
                pltpu.VMEM((3, block, block), BF16),
                pltpu.VMEM((3, block, block), BF16),
                pltpu.VMEM((bands + 2, block, block), BF16),
                pltpu.VMEM((bands + 2, block, block), BF16),
                dma((CHUNKS,)), dma((CHUNKS,)), dma((CHUNKS,)), dma((CHUNKS,)),
                dma((cols,)), dma((cols,)),
                dma((bands + 1, 2, depth)), dma((bands + 1, 2 * depth)), dma((bands + 1, rows)),
                dma((2,)), dma((rows,)), dma((1,)), dma((1,)), dma((2,)), dma((cols,)), dma((2,)), dma((2,)),
                dma((2,)), dma((2, 2, 2, depth)), dma((2, rows)), dma((6 + bands,)),
                dma((bands * block // TILE,)),
            ],
            compiler_params=pltpu.CompilerParams(
                collective_id=0, has_side_effects=True, vmem_limit_bytes=63 * 1024 * 1024
            ),
        )(covariance, left_ops, right_ops, edge_rows, edge_cols)

    return jax.shard_map(
        on_device,
        mesh=mesh,
        in_specs=(
            P("row", "col"),
            P("row", None, None, "col"),
            P("col", None, "row", None),
            P(None, "row", "col"),
            P("row", None, "col"),
        ),
        out_specs=P("row", "col"),
        check_vma=False,
    )
```
